128 devices in a mesh: seq: 8 (over y_lo, z), chan: 16 (over x, y_hi, core).
Axes of the slice: x: 4, y: 4 (y_hi: 2, y_lo: 2; y = y_hi * 2 + y_lo), z: 4, core: 2. Of those that a mesh axis runs over, the one named last changes fastest.
Arguments:
- resid: bfloat16 [16384, 4096], P('seq', 'chan'), may hold values from -1100 to 1100
- norm_gain: bfloat16 [4096], P('chan'), may hold values from 0.5 to 1.5
- feat_weight: bfloat16 [4096, 3, 4096], P(None, None, 'chan'), may hold values from -0.09375 to 0.09375
- short_filter: float32 [3, 3, 4096], P(None, None, 'chan'), may hold values from -3.5 to 3.5
- mr_filter: bfloat16 [128, 4096], P(None, 'chan'), may hold values from -0.5 to 0.5
- gates_lr: bfloat16 [16384, 2, 4096], P('seq', None, 'chan'), may hold values from -6 to 6
- decay_rate: float32 [16, 4096], P(None, 'chan'), may hold values from 1.2207031e-06 to 0.0333333333
- residue: float32 [16, 4096], P(None, 'chan'), may hold values from -1.5 to 1.5
- skip_gain: float32 [4096], P('chan'), may hold values from 0.5 to 1.5
Outputs:
- mixed: bfloat16 [16384, 4096], P('seq', 'chan')
The draws below stay inside these ranges and needn't reach their ends.
All inputs are finite; a program needn't handle non-finite values.
Results may differ from the reference program's by a relative error of at most 0.012.
Values may be sent and summed in bfloat16 or wider, within the bound.
A program may use at most 128 MiB of HBM per device.

```python
import math
import jax
import jax.numpy as jnp
from jax import lax

D = 4096
SHORT = 3
MR_LEN = 128
MODES = 16
LENGTH = 16384


def draw_resid(key, part):
    key_base, key_column, key_line = jax.random.split(key, 3)
    position = jnp.arange(D, dtype=jnp.float32) / max(D - 1, 1)
    column_scale = 10.0 ** jax.random.uniform(key_column, (D,), jnp.float32) * 3.0 ** (0.5 * position)
    line_scale = 10.0 ** jax.random.uniform(key_line, (LENGTH, 1), jnp.float32)
    base_values = jnp.clip(jax.random.normal(key_base, (LENGTH, D), jnp.float32), -6.0, 6.0)
    return (base_values * line_scale * column_scale[None]).astype(jnp.bfloat16)


def draw_decay_rate(key, part):
    key_slow = jax.random.fold_in(key, 2)
    lowest = math.log(0.02 / LENGTH)
    highest = math.log(1.0 / 30.0)
    return jnp.exp(jax.random.uniform(key_slow, (MODES, D), jnp.float32, lowest, highest))


def levels(rng, dims, pieces, least, largest):
    loudness = 1.0
    for dim, shards_of in pieces:
        steps = jax.random.uniform(jax.random.fold_in(jax.random.fold_in(rng, 6), dim), (shards_of,), jnp.float32, least / len(pieces), largest / len(pieces))
        loudness = loudness * jnp.repeat(jnp.exp(steps), dims[dim] // shards_of).reshape((-1,) + (1,) * (len(dims) - 1 - dim))
    return loudness


def gaussian(own_key, shape, spread, bound, cuts=(), held_as=jnp.bfloat16):
    drawn = jax.random.normal(own_key, shape, jnp.float32) * spread
    if len(cuts) > 0:
        drawn = levels(own_key, shape, cuts, -0.22, 0.18) * drawn
    return jnp.clip(drawn, min=-bound, max=bound).astype(held_as)


def setup_inputs(seed: int = 0) -> dict:
    arg_keys = jax.random.split(jax.random.key(seed), 10)
    resid = draw_resid(jax.random.fold_in(arg_keys[9], 71), 0)
    norm_gain = jnp.clip(1.0 + 0.1 * jax.random.normal(arg_keys[1], (D,), jnp.float32), 0.5, 1.5).astype(jnp.bfloat16)
    feat_weight = gaussian(arg_keys[2], (D, 3, D), D ** -0.5, 0.09375, ((2, 16),))
    short_filter = gaussian(arg_keys[3], (SHORT, 3, D), 0.6, 3.5, ((2, 16),), jnp.float32)
    mr_filter = gaussian(arg_keys[4], (MR_LEN, D), MR_LEN ** -0.5, 0.5, ((1, 16),))
    gates_lr = gaussian(arg_keys[5], (LENGTH, 2, D), 1.0, 6.0, ((0, 8), (2, 16)))
    decay_rate = draw_decay_rate(jax.random.fold_in(arg_keys[9], 71), 0)
    residue = gaussian(arg_keys[7], (MODES, D), 0.25, 1.5, ((1, 16),), jnp.float32)
    skip_gain = jnp.clip(0.5 + 1.0 * jax.random.uniform(arg_keys[8], (D,), jnp.float32) ** levels(arg_keys[8], (D,), ((0, 16),), -0.2, 0.2), 0.5, 1.5)
    return dict(resid=resid, norm_gain=norm_gain, feat_weight=feat_weight, short_filter=short_filter, mr_filter=mr_filter, gates_lr=gates_lr, decay_rate=decay_rate, residue=residue, skip_gain=skip_gain)


def grouped_causal(signal, taps_of_group, extra):
    group_width = 64
    group_count = D // group_width
    padded_len = 2 * LENGTH

    def one_group(inputs):
        signal_part = inputs[0]
        taps = taps_of_group(inputs[1:])
        spectrum = jnp.fft.rfft(signal_part, n=padded_len, axis=0) * jnp.fft.rfft(taps, n=padded_len, axis=0)
        return jnp.fft.irfft(spectrum, n=padded_len, axis=0)[:LENGTH]
    stacked = (signal.reshape(LENGTH, group_count, group_width).transpose(1, 0, 2),) + tuple((item.reshape(item.shape[0], group_count, group_width).transpose(1, 0, 2) for item in extra))
    result = lax.map(one_group, stacked)
    return result.transpose(1, 0, 2).reshape(LENGTH, D)

def long_conv(signal, decays, residues):
    times = jnp.arange(LENGTH, dtype=jnp.float32)
    weighted = residues * jnp.sqrt(-jnp.expm1(-2.0 * decays))

    def make_taps(parts):
        decay_part, weight_part = parts
        return lax.optimization_barrier(jnp.sum(weight_part[:, None, :] * jnp.exp(-decay_part[:, None, :] * times[None, :, None]), axis=0))
    return grouped_causal(signal, make_taps, (decays, weighted))

def medium_conv(signal, taps):

    def make_taps(parts):
        return parts[0]
    return grouped_causal(signal, make_taps, (taps,))

def reference(resid, norm_gain, feat_weight, short_filter, mr_filter, gates_lr, decay_rate, residue, skip_gain):
    values = resid.astype(jnp.float32)
    mean_square = lax.optimization_barrier(jnp.mean(values * values, axis=1, keepdims=True))
    normed = (values * lax.rsqrt(mean_square + 1e-05) * norm_gain.astype(jnp.float32)[None]).astype(jnp.bfloat16)
    projected = jnp.dot(normed.astype(jnp.float32), feat_weight.reshape(D, 3 * D).astype(jnp.float32), precision=lax.Precision.HIGHEST, preferred_element_type=jnp.float32)
    projected = projected.astype(jnp.bfloat16).reshape(LENGTH, 3, D)
    padded = jnp.concatenate([jnp.zeros((SHORT - 1, 3, D), projected.dtype), projected], axis=0)
    featured = jnp.zeros((LENGTH, 3, D), jnp.float32)
    for tap_index in range(SHORT):
        start_row = SHORT - 1 - tap_index
        featured = featured + padded[start_row:start_row + LENGTH].astype(jnp.float32) * short_filter[tap_index][None]
    product = (featured[:, 1] * featured[:, 2]).astype(jnp.bfloat16)
    medium = medium_conv(product.astype(jnp.float32), mr_filter.astype(jnp.float32))
    mixed_mr = (featured[:, 0] * medium).astype(jnp.bfloat16)
    gates = gates_lr.astype(jnp.float32)
    long_input = (gates[:, 1] * mixed_mr.astype(jnp.float32)).astype(jnp.bfloat16)
    long_out = long_conv(long_input.astype(jnp.float32), decay_rate, residue)
    return (gates[:, 0] * (long_out + skip_gain[None] * long_input.astype(jnp.float32))).astype(jnp.bfloat16)
```

```python
import functools

import jax
import jax.numpy as jnp
from jax import lax
from jax.experimental import pallas as pl
from jax.experimental.pallas import tpu as pltpu
from jax.sharding import PartitionSpec as P

norm_epsilon = 1e-05
lanes = 128
segs = 8
steps = 32
chunk = segs * steps
taps = 128
back = taps // steps
block = 16
group = 8


def sublane():
    return lax.broadcasted_iota(jnp.int32, (segs, lanes), 0)


def fill(row):
    return jnp.broadcast_to(row, (segs, lanes))


def lane_tile(i):
    return slice(i * lanes, (i + 1) * lanes)


def set_constants(groups, modes, sf_ref, mr_ref, decay_ref, weight_ref, skip_ref, sfb, fb, lam, skb, pw):
    for g in range(groups):
        cols = lane_tile(g)
        for s in range(3):
            for j in range(3):
                sfb[(s * groups + g) * 3 + j] = fill(sf_ref[j, s : s + 1, cols])
        skb[g] = fill(skip_ref[:, cols])

        def taps_at(t, carry):
            rows = mr_ref[pl.ds(pl.multiple_of(t * 16, 16), 16), cols].astype(jnp.float32)
            for i in range(16):
                fb[g, t * 16 + i] = fill(rows[i : i + 1])
            return carry

        lax.fori_loop(0, taps // 16, taps_at, 0)
        at = sublane().astype(jnp.float32) * float(steps)
        for m in range(modes):
            d = fill(decay_ref[m : m + 1, cols])
            lam[0, g, m] = jnp.exp(-d)
            lam[1, g, m] = fill(weight_ref[m : m + 1, cols])
            pw[0, g, m] = jnp.exp(d * (-1.0 * steps))
            pw[1, g, m] = jnp.exp(d * (-2.0 * steps))
            pw[2, g, m] = jnp.exp(d * (-4.0 * steps))
            pw[3, g, m] = jnp.exp(d * (-8.0 * steps))
            pw[4, g, m] = jnp.exp(-d * at)


def strided(ref, lead, r):
    return ref[lead, pl.ds(r, segs, stride=steps), :]


def short_part(groups, pj, tail, sfb, qs, pe):
    sub = sublane()
    for g in range(groups):
        names = [s * groups + g for s in range(3)]
        old = []
        for n in names:
            last = strided(pj, n, steps - 1)
            before = strided(pj, n, steps - 2)
            turned = (pltpu.roll(last, 1, 0), pltpu.roll(before, 1, 0))
            old.append(
                (
                    jnp.where(sub == 0, tail[n, 0], turned[0]),
                    jnp.where(sub == 0, tail[n, 1], turned[1]),
                )
            )
            tail[n, 0] = turned[0]
            tail[n, 1] = turned[1]

        def step(r, carry):
            after, featured = [], []
            for n, (one, two) in zip(names, carry):
                now = strided(pj, n, r)
                featured.append(sfb[n * 3] * now + sfb[n * 3 + 1] * one + sfb[n * 3 + 2] * two)
                after.append((now, one))
            product = (featured[1] * featured[2]).astype(jnp.bfloat16).astype(jnp.float32)
            qs[g, r] = featured[0]
            past = pe[g, taps + r]
            for i in range(1, back + 1):
                pe[g, taps - steps * i + r] = pltpu.roll(
                    jnp.where(sub >= segs - i, past, product), i, 0
                )
            pe[g, taps + r] = product
            return tuple(after)

        lax.fori_loop(0, steps, step, tuple(old), unroll=4)


def medium_part(groups, pe, fb, qs, gs, ls):
    for g in range(groups):

        def at_block(b, carry):
            def taps_at(t, sums):
                base = taps + b * block - t * group
                window = [pe[g, base - group + 1 + i] for i in range(block + group - 1)]
                sums = list(sums)
                for j in range(group):
                    tap = fb[g, t * group + j]
                    for i in range(block):
                        sums[i] = sums[i] + tap * window[group - 1 + i - j]
                return tuple(sums)

            zero = jnp.zeros((segs, lanes), jnp.float32)
            sums = lax.fori_loop(0, taps // group, taps_at, (zero,) * block)
            for i in range(block):
                r = b * block + i
                mixed = (qs[g, r] * sums[i]).astype(jnp.bfloat16).astype(jnp.float32)
                gate = strided(gs, g, r)
                ls[g, r] = (gate * mixed).astype(jnp.bfloat16).astype(jnp.float32)
            return carry

        lax.fori_loop(0, steps // block, at_block, 0)


def long_part(groups, modes, k, ls, lam, skb, pw, carry_ref, ys, inits):
    sub = sublane()
    for g in range(groups):

        def step(r, states):
            value = ls[g, r]
            total = skb[g] * value
            after = []
            for m in range(modes):
                state = lam[0, g, m] * states[m] + value
                total = total + lam[1, g, m] * state
                after.append(state)
            ys[k, g, r] = total
            return tuple(after)

        zero = jnp.zeros((segs, lanes), jnp.float32)
        ends = lax.fori_loop(0, steps, step, (zero,) * modes, unroll=2)
        for m in range(modes):
            scan = ends[m]
            for n in range(3):
                scan = scan + jnp.where(
                    sub >= 1 << n, pw[n, g, m] * pltpu.roll(scan, 1 << n, 0), 0.0
                )
            carry = carry_ref[g, m]
            inits[k, g, m] = (
                jnp.where(sub == 0, 0.0, pltpu.roll(scan, 1, 0)) + pw[4, g, m] * carry
            )
            carry_ref[g, m] = fill(scan[segs - 1 : segs]) + pw[3, g, m] * carry


def finish_part(groups, modes, k, incoming, lam, pw, ys, inits, gs, outs):
    for g in range(groups):
        starts = []
        for m in range(modes):
            start = incoming[g, m]
            starts.append(lam[1, g, m] * (inits[k, g, m] + pw[4, g, m] * start))
            incoming[g, m] = pw[3, g, m] * start

        def step(r, states):
            total = ys[k, g, r]
            after = []
            for m in range(modes):
                state = lam[0, g, m] * states[m]
                total = total + state
                after.append(state)
            outs[g, pl.ds(r, segs, stride=steps), :] = strided(gs, g, r) * total
            return tuple(after)

        lax.fori_loop(0, steps, step, tuple(starts), unroll=2)


def load_gates(groups, which, k, gates_ref, gs):
    rows = pl.ds(pl.multiple_of(k * chunk, chunk), chunk)
    for g in range(groups):
        gs[g] = gates_ref[which, rows, lane_tile(g)].astype(jnp.float32)


def local_kernel(
    groups, modes, chunks,
    proj_ref, halo_ref, sf_ref, mr_ref, gates_ref, decay_ref, weight_ref, skip_ref,
    ys, inits, ends_ref,
    pj, tail, sfb, qs, pe, fb, gs, ls, lam, skb, pw, carry_ref,
):
    set_constants(groups, modes, sf_ref, mr_ref, decay_ref, weight_ref, skip_ref, sfb, fb, lam, skb, pw)
    carry_ref[...] = jnp.zeros_like(carry_ref)
    tail[...] = jnp.zeros_like(tail)
    pe[...] = jnp.zeros_like(pe)
    for n in range(3 * groups):
        pj[n] = halo_ref[:, lane_tile(n)].astype(jnp.float32)
    short_part(groups, pj, tail, sfb, qs, pe)

    def body(k, c):
        rows = pl.ds(pl.multiple_of(k * chunk, chunk), chunk)
        for n in range(3 * groups):
            pj[n] = proj_ref[rows, lane_tile(n)].astype(jnp.float32)
        short_part(groups, pj, tail, sfb, qs, pe)
        load_gates(groups, 1, k, gates_ref, gs)
        medium_part(groups, pe, fb, qs, gs, ls)
        long_part(groups, modes, k, ls, lam, skb, pw, carry_ref, ys, inits)
        return c

    lax.fori_loop(0, chunks, body, 0)
    for g in range(groups):
        for m in range(modes):
            ends_ref[g, m : m + 1, :] = carry_ref[g, m, 0:1, :]


def finish_kernel(
    groups, modes, chunks, peers,
    ends_ref, place_ref, ys, inits, gates_ref, decay_ref, weight_ref,
    out_ref,
    lam, pw, incoming, gs, outs,
):
    at = sublane().astype(jnp.float32) * float(steps)
    for g in range(groups):
        cols = lane_tile(g)
        for m in range(modes):
            d = fill(decay_ref[m : m + 1, cols])
            lam[0, g, m] = jnp.exp(-d)
            lam[1, g, m] = fill(weight_ref[m : m + 1, cols])
            pw[3, g, m] = jnp.exp(d * (-8.0 * steps))
            pw[4, g, m] = jnp.exp(-d * at)
        total = jnp.zeros((modes, lanes), jnp.float32)
        d = decay_ref[:, cols]
        for p in range(peers):
            gap = place_ref[p : p + 1, :]
            total = total + jnp.where(
                gap >= 0.0, jnp.exp(-d * (jnp.maximum(gap, 0.0) * float(chunk * chunks))), 0.0
            ) * ends_ref[p, g]
        for m in range(modes):
            incoming[g, m] = fill(total[m : m + 1])

    def body(k, c):
        load_gates(groups, 0, k, gates_ref, gs)
        finish_part(groups, modes, k, incoming, lam, pw, ys, inits, gs, outs)
        rows = pl.ds(pl.multiple_of(k * chunk, chunk), chunk)
        for g in range(groups):
            out_ref[rows, lane_tile(g)] = outs[g].astype(jnp.bfloat16)
        return c

    lax.fori_loop(0, chunks, body, 0)


def in_vmem(n):
    return [pl.BlockSpec(memory_space=pltpu.VMEM)] * n


def vregs(*lead):
    return pltpu.VMEM(lead + (segs, lanes), jnp.float32)


def local_call(proj, halo, short_filter, mr_filter, gates, decays, weights, skip):
    length = proj.shape[0]
    modes, width = decays.shape
    groups, chunks = width // lanes, length // chunk
    f32 = jnp.float32
    return pl.pallas_call(
        functools.partial(local_kernel, groups, modes, chunks),
        out_shape=(
            jax.ShapeDtypeStruct((chunks, groups, steps, segs, lanes), f32),
            jax.ShapeDtypeStruct((chunks, groups, modes, segs, lanes), f32),
            jax.ShapeDtypeStruct((groups, modes, lanes), f32),
        ),
        in_specs=in_vmem(8),
        out_specs=tuple(in_vmem(3)),
        scratch_shapes=[
            pltpu.VMEM((3 * groups, chunk, lanes), f32),
            vregs(3 * groups, 2),
            vregs(9 * groups),
            vregs(groups, steps),
            vregs(groups, taps + steps),
            vregs(groups, taps),
            pltpu.VMEM((groups, chunk, lanes), f32),
            vregs(groups, steps),
            vregs(2, groups, modes),
            vregs(groups),
            vregs(5, groups, modes),
            vregs(groups, modes),
        ],
        compiler_params=pltpu.CompilerParams(vmem_limit_bytes=56 << 20),
    )(proj, halo, short_filter, mr_filter, gates, decays, weights, skip)


def finish_call(ends, place, ys, inits, gates, decays, weights):
    chunks = ys.shape[0]
    modes, width = decays.shape
    groups = width // lanes
    return pl.pallas_call(
        functools.partial(finish_kernel, groups, modes, chunks, ends.shape[0]),
        out_shape=jax.ShapeDtypeStruct((chunks * chunk, width), jnp.bfloat16),
        in_specs=in_vmem(7),
        out_specs=pl.BlockSpec(memory_space=pltpu.VMEM),
        scratch_shapes=[
            vregs(2, groups, modes),
            vregs(5, groups, modes),
            vregs(groups, modes),
            pltpu.VMEM((groups, chunk, lanes), jnp.float32),
            pltpu.VMEM((groups, chunk, lanes), jnp.float32),
        ],
        compiler_params=pltpu.CompilerParams(vmem_limit_bytes=56 << 20),
    )(ends, place, ys, inits, gates, decays, weights)


def shifted(value, axis, by):
    peers = lax.axis_size(axis)
    pairs = [(i, i + by) for i in range(peers) if 0 <= i + by < peers]
    return lax.ppermute(value, axis, pairs)


def on_device(
    resid, norm_gain, feat_weight, short_filter, mr_filter, gates_lr, decay_rate, residue, skip_gain
):
    tokens, channels = resid.shape
    width = feat_weight.shape[0]
    values = resid.astype(jnp.float32)
    squares = lax.psum(jnp.sum(values * values, axis=1), "chan")
    inv_scale = lax.rsqrt(squares / width + norm_epsilon)
    normed = (values * inv_scale[:, None] * norm_gain.astype(jnp.float32)[None]).astype(jnp.bfloat16)
    rows = lax.all_gather(normed, "chan", axis=1, tiled=True)
    projected = jnp.concatenate(
        [
            jnp.dot(rows, feat_weight[:, s], preferred_element_type=jnp.float32).astype(jnp.bfloat16)
            for s in range(3)
        ],
        axis=1,
    )
    halo = shifted(projected[tokens - chunk :], "seq", 1)
    gates = jnp.transpose(gates_lr, (1, 0, 2))
    weights = residue * jnp.sqrt(-jnp.expm1(-2.0 * decay_rate))
    ys, inits, ends = local_call(
        projected, halo, short_filter, mr_filter, gates, decay_rate, weights, skip_gain[None]
    )
    all_ends = lax.all_gather(ends, "seq")
    peers = lax.axis_size("seq")
    gap = lax.axis_index("seq") - 1 - jnp.arange(peers)
    place = jnp.broadcast_to(gap.astype(jnp.float32)[:, None], (peers, lanes))
    return finish_call(all_ends, place, ys, inits, gates, decay_rate, weights)


def solution(mesh):
    in_specs = (
        P("seq", "chan"),
        P("chan"),
        P(None, None, "chan"),
        P(None, None, "chan"),
        P(None, "chan"),
        P("seq", None, "chan"),
        P(None, "chan"),
        P(None, "chan"),
        P("chan"),
    )
    return jax.shard_map(
        on_device, mesh=mesh, in_specs=in_specs, out_specs=P("seq", "chan"), check_vma=False
    )
```

```python
import functools

import jax
import jax.numpy as jnp
from jax import lax
from jax.experimental import pallas as pl
from jax.experimental.pallas import tpu as pltpu
from jax.sharding import PartitionSpec as P

norm_epsilon = 1e-05
lanes = 128
segs = 8
steps = 32
chunk = segs * steps
taps = 128
back = taps // steps
block = 16
group = 8


def sublane():
    return lax.broadcasted_iota(jnp.int32, (segs, lanes), 0)


def fill(row):
    return jnp.broadcast_to(row, (segs, lanes))


def lane_tile(i):
    return slice(i * lanes, (i + 1) * lanes)


def set_constants(groups, modes, sf_ref, mr_ref, decay_ref, weight_ref, skip_ref, sfb, fb, lam, skb, pw):
    for g in range(groups):
        cols = lane_tile(g)
        for s in range(3):
            for j in range(3):
                sfb[(s * groups + g) * 3 + j] = fill(sf_ref[j, s : s + 1, cols])
        skb[g] = fill(skip_ref[:, cols])

        def taps_at(t, carry):
            rows = mr_ref[pl.ds(pl.multiple_of(t * 16, 16), 16), cols].astype(jnp.float32)
            for i in range(16):
                fb[g, t * 16 + i] = fill(rows[i : i + 1])
            return carry

        lax.fori_loop(0, taps // 16, taps_at, 0)
        at = sublane().astype(jnp.float32) * float(steps)
        for m in range(modes):
            d = fill(decay_ref[m : m + 1, cols])
            lam[0, g, m] = jnp.exp(-d)
            lam[1, g, m] = fill(weight_ref[m : m + 1, cols])
            pw[0, g, m] = jnp.exp(d * (-1.0 * steps))
            pw[1, g, m] = jnp.exp(d * (-2.0 * steps))
            pw[2, g, m] = jnp.exp(d * (-4.0 * steps))
            pw[3, g, m] = jnp.exp(d * (-8.0 * steps))
            pw[4, g, m] = jnp.exp(-d * at)


def strided(ref, lead, r):
    return ref[lead, pl.ds(r, segs, stride=steps), :]


def short_part(groups, pj, tail, sfb, qs, pe):
    sub = sublane()
    for g in range(groups):
        names = [s * groups + g for s in range(3)]
        old = []
        for n in names:
            last = strided(pj, n, steps - 1)
            before = strided(pj, n, steps - 2)
            turned = (pltpu.roll(last, 1, 0), pltpu.roll(before, 1, 0))
            old.append(
                (
                    jnp.where(sub == 0, tail[n, 0], turned[0]),
                    jnp.where(sub == 0, tail[n, 1], turned[1]),
                )
            )
            tail[n, 0] = turned[0]
            tail[n, 1] = turned[1]

        def step(r, carry):
            after, featured = [], []
            for n, (one, two) in zip(names, carry):
                now = strided(pj, n, r)
                featured.append(sfb[n * 3] * now + sfb[n * 3 + 1] * one + sfb[n * 3 + 2] * two)
                after.append((now, one))
            product = (featured[1] * featured[2]).astype(jnp.bfloat16).astype(jnp.float32)
            qs[g, r] = featured[0]
            past = pe[g, taps + r]
            for i in range(1, back + 1):
                pe[g, taps - steps * i + r] = pltpu.roll(
                    jnp.where(sub >= segs - i, past, product), i, 0
                )
            pe[g, taps + r] = product
            return tuple(after)

        lax.fori_loop(0, steps, step, tuple(old), unroll=4)


def medium_part(groups, pe, fb, qs, gs, ls):
    for g in range(groups):

        def at_block(b, carry):
            def taps_at(t, sums):
                base = taps + b * block - t * group
                window = [pe[g, base - group + 1 + i] for i in range(block + group - 1)]
                sums = list(sums)
                for j in range(group):
                    tap = fb[g, t * group + j]
                    for i in range(block):
                        sums[i] = sums[i] + tap * window[group - 1 + i - j]
                return tuple(sums)

            zero = jnp.zeros((segs, lanes), jnp.float32)
            sums = lax.fori_loop(0, taps // group, taps_at, (zero,) * block)
            for i in range(block):
                r = b * block + i
                mixed = (qs[g, r] * sums[i]).astype(jnp.bfloat16).astype(jnp.float32)
                gate = strided(gs, g, r)
                ls[g, r] = (gate * mixed).astype(jnp.bfloat16).astype(jnp.float32)
            return carry

        lax.fori_loop(0, steps // block, at_block, 0)


def long_part(groups, modes, k, ls, lam, skb, pw, carry_ref, ys, inits):
    sub = sublane()
    for g in range(groups):

        def step(r, states):
            value = ls[g, r]
            total = skb[g] * value
            after = []
            for m in range(modes):
                state = lam[0, g, m] * states[m] + value
                total = total + lam[1, g, m] * state
                after.append(state)
            ys[k, g, r] = total
            return tuple(after)

        zero = jnp.zeros((segs, lanes), jnp.float32)
        ends = lax.fori_loop(0, steps, step, (zero,) * modes, unroll=2)
        for m in range(modes):
            scan = ends[m]
            for n in range(3):
                scan = scan + jnp.where(
                    sub >= 1 << n, pw[n, g, m] * pltpu.roll(scan, 1 << n, 0), 0.0
                )
            carry = carry_ref[g, m]
            inits[k, g, m] = (
                jnp.where(sub == 0, 0.0, pltpu.roll(scan, 1, 0)) + pw[4, g, m] * carry
            )
            carry_ref[g, m] = fill(scan[segs - 1 : segs]) + pw[3, g, m] * carry


def finish_part(groups, modes, k, incoming, lam, pw, ys, inits, gs, outs):
    for g in range(groups):
        starts = []
        for m in range(modes):
            start = incoming[g, m]
            starts.append(lam[1, g, m] * (inits[k, g, m] + pw[4, g, m] * start))
            incoming[g, m] = pw[3, g, m] * start

        def step(r, states):
            total = ys[k, g, r]
            after = []
            for m in range(modes):
                state = lam[0, g, m] * states[m]
                total = total + state
                after.append(state)
            outs[g, pl.ds(r, segs, stride=steps), :] = strided(gs, g, r) * total
            return tuple(after)

        lax.fori_loop(0, steps, step, tuple(starts), unroll=2)


def load_gates(groups, which, k, gates_ref, gs):
    rows = pl.ds(pl.multiple_of(k * chunk, chunk), chunk)
    for g in range(groups):
        gs[g] = gates_ref[which, rows, lane_tile(g)].astype(jnp.float32)


MESH = pl.DeviceIdType.MESH
kinds = 17
halo_rows = taps + 16


def columns(owner):
    return pl.ds(pl.multiple_of(owner * 256, 256), 256)


class Mover:
    def __init__(self, chunks, resid_ref, rows_ref, send_sem, recv_sem, own_sem):
        self.chunks = chunks
        self.resid, self.rows = resid_ref, rows_ref
        self.send_sem, self.recv_sem, self.own_sem = send_sem, recv_sem, own_sem
        me = lax.axis_index("chan")
        core, pair, x = lax.rem(me, 2), lax.rem(me // 2, 2), me // 4
        right, left, far = lax.rem(x + 1, 4), lax.rem(x + 3, 4), lax.rem(x + 2, 4)
        other = 1 - pair

        def at(x, y):
            return x * 4 + y * 2 + core

        twin = x * 4 + pair * 2 + (1 - core)
        self.me, self.twin = me, twin
        whole, first, second = (0, chunk), (0, chunk // 2), (chunk // 2, chunk // 2)
        here = [
            at(x, pair), at(left, pair), at(right, pair), at(x, other),
            at(far, pair), at(left, other), at(right, other), at(far, other),
        ]
        self.table = {
            0: (at(right, pair), here[0], at(left, pair), whole),
            1: (at(left, pair), here[0], at(right, pair), whole),
            2: (at(x, other), here[0], at(x, other), whole),
            3: (at(right, pair), at(left, pair), at(far, pair), first),
            4: (at(left, pair), at(right, pair), at(far, pair), second),
            5: (at(right, pair), at(x, other), at(left, other), whole),
            6: (at(left, pair), at(x, other), at(right, other), whole),
            7: (at(right, pair), at(left, other), at(far, other), first),
            8: (at(left, pair), at(right, other), at(far, other), second),
        }
        flip = 1 - 2 * core
        for n, block in enumerate(here):
            self.table[9 + n] = (twin, block, block + flip, whole)

    def token_rows(self, q):
        return pl.ds(pl.multiple_of(lax.rem(q + self.chunks - 1, self.chunks) * chunk, chunk), chunk)

    def make(self, q, kind):
        target, sent, _, (begin, count) = self.table[kind]
        place = self.rows.at[q, pl.ds(begin, count), columns(sent)]
        source = self.resid.at[self.token_rows(q), :] if kind in (0, 1, 2, 9) else place
        return pltpu.make_async_remote_copy(
            src_ref=source,
            dst_ref=place,
            send_sem=self.send_sem.at[q, kind],
            recv_sem=self.recv_sem.at[q, kind],
            device_id={"chan": target},
            device_id_type=MESH,
        )

    def start(self, q, *which):
        for kind in which:
            self.make(q, kind).start()

    def sent(self, q):
        for kind in range(kinds):
            self.make(q, kind).wait_send()

    def arrived(self, q, *which):
        for kind in which:
            target, _, received, (begin, count) = self.table[kind]
            place = self.rows.at[q, pl.ds(begin, count), columns(received)]
            pltpu.make_async_remote_copy(
                src_ref=place,
                dst_ref=place,
                send_sem=self.send_sem.at[q, kind],
                recv_sem=self.recv_sem.at[q, kind],
                device_id={"chan": target},
                device_id_type=MESH,
            ).wait_recv()

    def own(self, q):
        return pltpu.make_async_copy(
            self.resid.at[self.token_rows(q), :],
            self.rows.at[q, :, columns(self.me)],
            self.own_sem.at[q],
        )

    def stage_1(self, q):
        self.start(q, 0, 1, 2, 9)
        self.own(q).start()

    def stage_2(self, q):
        self.arrived(q, 2)
        self.start(q, 5, 6, 12)
        self.arrived(q, 0)
        self.start(q, 3, 10)
        self.arrived(q, 1)
        self.start(q, 4, 11)

    def stage_3(self, q):
        self.arrived(q, 5)
        self.start(q, 7, 14)
        self.arrived(q, 6)
        self.start(q, 8, 15)
        self.arrived(q, 3, 4)
        self.start(q, 13)

    def stage_4(self, q):
        self.arrived(q, 7, 8)
        self.start(q, 16)

    def stage_5(self, q):
        self.own(q).wait()
        self.arrived(q, 9, 10, 11, 12, 13, 14, 15, 16)


def scale_weights(groups, peers, gains, wts):
    def body(j, c):
        for h in range(2):
            row = gains[j, :, lane_tile(h)]
            column = jnp.transpose(jnp.broadcast_to(row, (lanes, lanes)))
            rows = pl.ds(pl.multiple_of(j * 256 + h * lanes, lanes), lanes)
            for s in range(3):
                for g in range(groups):
                    value = wts[s, rows, lane_tile(g)].astype(jnp.float32)
                    wts[s, rows, lane_tile(g)] = (value * column).astype(jnp.bfloat16)
        return c

    lax.fori_loop(0, peers, body, 0)


def project(groups, q, width, rows_ref, wts, pj):
    def square(t, total):
        value = rows_ref[q, :, pl.ds(pl.multiple_of(t * lanes, lanes), lanes)].astype(jnp.float32)
        return total + value * value

    total = lax.fori_loop(
        0, width // lanes, square, jnp.zeros((chunk, lanes), jnp.float32), unroll=2
    )
    scale = lax.rsqrt(jnp.sum(total, axis=1, keepdims=True) / width + norm_epsilon)
    for s in range(3):
        value = jnp.dot(rows_ref[q], wts[s], preferred_element_type=jnp.float32) * scale
        value = value.astype(jnp.bfloat16).astype(jnp.float32)
        for g in range(groups):
            pj[s * groups + g] = value[:, lane_tile(g)]


def fused_kernel(
    groups, modes, chunks, sides, peers,
    resid_ref, gain_ref, weight_hbm, sf_ref, mr_ref, gates_ref, decay_ref, modal_ref, skip_ref,
    out_ref,
    rows_ref, wts, gains, pj, pj_last, halo_out, halo_in, states, outs,
    tail, sfb, qs, pe, fb, gs, ls, lam, skb, pw, carry_ref, incoming, ys, inits,
    send_sem, recv_sem, own_sem, gain_send, gain_recv, state_send, state_recv, halo_sem, weight_sem,
):
    me, part = lax.axis_index("chan"), lax.axis_index("seq")
    load = pltpu.make_async_copy(weight_hbm, wts, weight_sem)
    load.start()

    barrier = pltpu.get_barrier_semaphore()
    for o in range(1, sides):
        pl.semaphore_signal(barrier, inc=1, device_id={"chan": lax.rem(me + o, sides)}, device_id_type=MESH)
    for o in range(1, peers):
        pl.semaphore_signal(barrier, inc=1, device_id={"seq": lax.rem(part + o, peers)}, device_id_type=MESH)
    pl.semaphore_wait(barrier, sides + peers - 2)

    mover = Mover(chunks, resid_ref, rows_ref, send_sem, recv_sem, own_sem)
    mover.stage_1(0)

    def gain_copy(o):
        return pltpu.make_async_remote_copy(
            src_ref=gain_ref, dst_ref=gains.at[me],
            send_sem=gain_send.at[o], recv_sem=gain_recv.at[o],
            device_id={"chan": lax.rem(me + o, sides)}, device_id_type=MESH,
        )

    for o in range(1, sides):
        gain_copy(o).start()
    mover.stage_1(1)
    set_constants(groups, modes, sf_ref, mr_ref, decay_ref, modal_ref, skip_ref, sfb, fb, lam, skb, pw)
    carry_ref[...] = jnp.zeros_like(carry_ref)
    tail[...] = jnp.zeros_like(tail)
    pe[...] = jnp.zeros_like(pe)
    mover.stage_2(0)
    mover.stage_1(2)
    mover.stage_2(1)
    mover.stage_3(0)
    own_gain = pltpu.make_async_copy(gain_ref, gains.at[me], weight_sem)
    load.wait()
    own_gain.start()
    own_gain.wait()
    for o in range(1, sides):
        source = lax.rem(me + sides - o, sides)
        pltpu.make_async_remote_copy(
            src_ref=gain_ref, dst_ref=gains.at[source],
            send_sem=gain_send.at[o], recv_sem=gain_recv.at[o],
            device_id={"chan": source}, device_id_type=MESH,
        ).wait_recv()
    scale_weights(groups, sides, gains, wts)
    mover.stage_1(3)
    mover.stage_2(2)
    mover.stage_3(1)
    mover.stage_4(0)
    mover.stage_1(4)

    def halo_copy():
        return pltpu.make_async_remote_copy(
            src_ref=halo_out, dst_ref=halo_in,
            send_sem=halo_sem.at[0], recv_sem=halo_sem.at[1],
            device_id={"seq": lax.rem(part + 1, peers)}, device_id_type=MESH,
        )

    def body(q, c):
        @pl.when(q < chunks)
        def _():
            mover.stage_5(q)

        @pl.when(q + 1 < chunks)
        def _():
            mover.stage_4(q + 1)

        @pl.when(q + 2 < chunks)
        def _():
            mover.stage_3(q + 2)

        @pl.when(q < chunks)
        def _():
            project(groups, q, sides * 256, rows_ref, wts, pj)

        @pl.when(q + 3 < chunks)
        def _():
            mover.stage_2(q + 3)

        @pl.when(q + 5 < chunks)
        def _():
            mover.stage_1(q + 5)

        @pl.when(q == 0)
        def _():
            for n in range(3 * groups):
                pj_last[n] = pj[n]
                halo_out[:, lane_tile(n)] = pj[n, chunk - halo_rows :, :].astype(jnp.bfloat16)
            halo_copy().start()

        @pl.when(q == 1)
        def _():
            halo_copy().wait()
            seen = jnp.where(part > 0, 1.0, 0.0)
            for n in range(3 * groups):
                outs[n] = jnp.zeros((chunk, lanes), jnp.float32)
                outs[n, chunk - halo_rows :, :] = halo_in[:, lane_tile(n)].astype(jnp.float32) * seen
            short_part(groups, outs, tail, sfb, qs, pe)

        @pl.when(q == chunks)
        def _():
            pj[...] = pj_last[...]

        @pl.when(q > 0)
        def _():
            k = q - 1
            short_part(groups, pj, tail, sfb, qs, pe)
            load_gates(groups, 1, k, gates_ref, gs)
            medium_part(groups, pe, fb, qs, gs, ls)
            long_part(groups, modes, k, ls, lam, skb, pw, carry_ref, ys, inits)

        return c

    lax.fori_loop(0, chunks + 1, body, 0)

    for g in range(groups):
        for m in range(modes):
            states[0, g, m : m + 1, :] = carry_ref[g, m, 0:1, :]

    def state_copy(o):
        return pltpu.make_async_remote_copy(
            src_ref=states.at[0], dst_ref=states.at[o],
            send_sem=state_send.at[o], recv_sem=state_recv.at[o],
            device_id={"seq": lax.rem(part + o, peers)}, device_id_type=MESH,
        )

    for o in range(1, peers):
        state_copy(o).start()

    def drain(q, c):
        mover.sent(q)
        return c

    lax.fori_loop(0, chunks, drain, 0)
    for o in range(1, sides):
        gain_copy(o).wait_send()
    for o in range(1, peers):
        state_copy(o).wait()
    for g in range(groups):
        total = jnp.zeros((modes, lanes), jnp.float32)
        d = decay_ref[:, lane_tile(g)]
        for o in range(1, peers):
            weight = jnp.exp(d * (-1.0 * chunk * chunks * (o - 1)))
            total = total + jnp.where(part >= o, weight, 0.0) * states[o, g]
        for m in range(modes):
            incoming[g, m] = fill(total[m : m + 1])

    def finish(k, c):
        load_gates(groups, 0, k, gates_ref, gs)
        finish_part(groups, modes, k, incoming, lam, pw, ys, inits, gs, outs)
        rows = pl.ds(pl.multiple_of(k * chunk, chunk), chunk)
        for g in range(groups):
            out_ref[rows, lane_tile(g)] = outs[g].astype(jnp.bfloat16)
        return c

    lax.fori_loop(0, chunks, finish, 0)


def in_vmem(n):
    return [pl.BlockSpec(memory_space=pltpu.VMEM)] * n


def vregs(*lead):
    return pltpu.VMEM(lead + (segs, lanes), jnp.float32)


def fused_call(resid, gain, weight, short_filter, mr_filter, gates, decays, modal, skip):
    length, width = resid.shape
    modes = decays.shape[0]
    groups, chunks = width // lanes, length // chunk
    sides, peers = lax.axis_size("chan"), lax.axis_size("seq")
    f32, bf16 = jnp.float32, jnp.bfloat16
    dma = pltpu.SemaphoreType.DMA
    anywhere = pl.BlockSpec(memory_space=pl.ANY)
    vmem = pl.BlockSpec(memory_space=pltpu.VMEM)
    return pl.pallas_call(
        functools.partial(fused_kernel, groups, modes, chunks, sides, peers),
        out_shape=jax.ShapeDtypeStruct((length, width), bf16),
        in_specs=[anywhere, vmem, anywhere] + [vmem] * 6,
        out_specs=vmem,
        scratch_shapes=[
            pltpu.VMEM((chunks, chunk, sides * width), bf16),
            pltpu.VMEM((3, sides * width, width), bf16),
            pltpu.VMEM((sides, 1, width), f32),
            pltpu.VMEM((3 * groups, chunk, lanes), f32),
            pltpu.VMEM((3 * groups, chunk, lanes), f32),
            pltpu.VMEM((halo_rows, 3 * width), bf16),
            pltpu.VMEM((halo_rows, 3 * width), bf16),
            pltpu.VMEM((peers, groups, modes, lanes), f32),
            pltpu.VMEM((3 * groups, chunk, lanes), f32),
            vregs(3 * groups, 2),
            vregs(9 * groups),
            vregs(groups, steps),
            vregs(groups, taps + steps),
            vregs(groups, taps),
            pltpu.VMEM((groups, chunk, lanes), f32),
            vregs(groups, steps),
            vregs(2, groups, modes),
            vregs(groups),
            vregs(5, groups, modes),
            vregs(groups, modes),
            vregs(groups, modes),
            vregs(chunks, groups, steps),
            vregs(chunks, groups, modes),
            dma((chunks, kinds)),
            dma((chunks, kinds)),
            dma((chunks,)),
            dma((sides,)),
            dma((sides,)),
            dma((peers,)),
            dma((peers,)),
            dma((2,)),
            dma,
        ],
        compiler_params=pltpu.CompilerParams(
            vmem_limit_bytes=60 << 20, collective_id=0, has_side_effects=True
        ),
    )(resid, gain, weight, short_filter, mr_filter, gates, decays, modal, skip)


def on_device(
    resid, norm_gain, feat_weight, short_filter, mr_filter, gates_lr, decay_rate, residue, skip_gain
):
    modal = residue * jnp.sqrt(-jnp.expm1(-2.0 * decay_rate))
    return fused_call(
        resid,
        norm_gain.astype(jnp.float32)[None],
        jnp.transpose(feat_weight, (1, 0, 2)),
        short_filter,
        mr_filter,
        jnp.transpose(gates_lr, (1, 0, 2)),
        decay_rate,
        modal,
        skip_gain[None],
    )


def solution(mesh):
    in_specs = (
        P("seq", "chan"),
        P("chan"),
        P(None, None, "chan"),
        P(None, None, "chan"),
        P(None, "chan"),
        P("seq", None, "chan"),
        P(None, "chan"),
        P(None, "chan"),
        P("chan"),
    )
    return jax.shard_map(
        on_device, mesh=mesh, in_specs=in_specs, out_specs=P("seq", "chan"), check_vma=False
    )
```

```python
import functools

import jax
import jax.numpy as jnp
from jax import lax
from jax.experimental import pallas as pl
from jax.experimental.pallas import tpu as pltpu
from jax.sharding import PartitionSpec as P

norm_epsilon = 1e-05
lanes = 128
segs = 8
steps = 32
chunk = segs * steps
taps = 128
back = taps // steps
block = 16
group = 8


def sublane():
    return lax.broadcasted_iota(jnp.int32, (segs, lanes), 0)


def fill(row):
    return jnp.broadcast_to(row, (segs, lanes))


def lane_tile(i):
    return slice(i * lanes, (i + 1) * lanes)


def modal_weights(decay, residue):
    x = decay * 2.0
    small = x * (1.0 - x / 2.0 * (1.0 - x / 3.0 * (1.0 - x / 4.0 * (1.0 - x / 5.0 * (1.0 - x / 6.0)))))
    return residue * jnp.sqrt(jnp.where(x < 0.125, small, 1.0 - jnp.exp(-x)))


def set_constants(groups, modes, sf_ref, mr_ref, decay_ref, residue_ref, skip, sfb, fb, lam, skb, pw):
    for g in range(groups):
        cols = lane_tile(g)
        for s in range(3):
            for j in range(3):
                sfb[(s * groups + g) * 3 + j] = fill(sf_ref[j, s : s + 1, cols])
        skb[g] = fill(skip[:, cols])

        def taps_at(t, carry):
            rows = mr_ref[pl.ds(pl.multiple_of(t * 16, 16), 16), cols].astype(jnp.float32)
            for i in range(16):
                fb[g, t * 16 + i] = fill(rows[i : i + 1])
            return carry

        lax.fori_loop(0, taps // 16, taps_at, 0)
        at = sublane().astype(jnp.float32) * float(steps)
        modal = modal_weights(decay_ref[:, cols], residue_ref[:, cols])
        for m in range(modes):
            d = fill(decay_ref[m : m + 1, cols])
            lam[0, g, m] = jnp.exp(-d)
            lam[1, g, m] = fill(modal[m : m + 1])
            pw[0, g, m] = jnp.exp(d * (-1.0 * steps))
            pw[1, g, m] = jnp.exp(d * (-2.0 * steps))
            pw[2, g, m] = jnp.exp(d * (-4.0 * steps))
            pw[3, g, m] = jnp.exp(d * (-8.0 * steps))
            pw[4, g, m] = jnp.exp(-d * at)


def strided(ref, lead, r):
    return ref[lead, pl.ds(r, segs, stride=steps), :]


def short_part(groups, pj, tail, sfb, qs, pe):
    sub = sublane()
    for g in range(groups):
        names = [s * groups + g for s in range(3)]
        old = []
        for n in names:
            last = strided(pj, n, steps - 1)
            before = strided(pj, n, steps - 2)
            turned = (pltpu.roll(last, 1, 0), pltpu.roll(before, 1, 0))
            old.append(
                (
                    jnp.where(sub == 0, tail[n, 0], turned[0]),
                    jnp.where(sub == 0, tail[n, 1], turned[1]),
                )
            )
            tail[n, 0] = turned[0]
            tail[n, 1] = turned[1]

        def step(r, carry):
            after, featured = [], []
            for n, (one, two) in zip(names, carry):
                now = strided(pj, n, r)
                featured.append(sfb[n * 3] * now + sfb[n * 3 + 1] * one + sfb[n * 3 + 2] * two)
                after.append((now, one))
            product = (featured[1] * featured[2]).astype(jnp.bfloat16).astype(jnp.float32)
            qs[g, r] = featured[0]
            past = pe[g, taps + r]
            for i in range(1, back + 1):
                pe[g, taps - steps * i + r] = pltpu.roll(
                    jnp.where(sub >= segs - i, past, product), i, 0
                )
            pe[g, taps + r] = product
            return tuple(after)

        lax.fori_loop(0, steps, step, tuple(old), unroll=4)


def medium_part(groups, pe, fb, qs, gs, ls):
    for g in range(groups):

        def at_block(b, carry):
            def taps_at(t, sums):
                base = taps + b * block - t * group
                window = [pe[g, base - group + 1 + i] for i in range(block + group - 1)]
                sums = list(sums)
                for j in range(group):
                    tap = fb[g, t * group + j]
                    for i in range(block):
                        sums[i] = sums[i] + tap * window[group - 1 + i - j]
                return tuple(sums)

            zero = jnp.zeros((segs, lanes), jnp.float32)
            sums = lax.fori_loop(0, taps // group, taps_at, (zero,) * block)
            for i in range(block):
                r = b * block + i
                mixed = (qs[g, r] * sums[i]).astype(jnp.bfloat16).astype(jnp.float32)
                gate = gate_at(gs, groups, g, 1, r)
                ls[g, r] = (gate * mixed).astype(jnp.bfloat16).astype(jnp.float32)
            return carry

        lax.fori_loop(0, steps // block, at_block, 0)


def long_part(groups, modes, k, ls, lam, skb, pw, carry_ref, ys, inits):
    sub = sublane()
    for g in range(groups):

        def step(r, states):
            value = ls[g, r]
            total = skb[g] * value
            after = []
            for m in range(modes):
                state = lam[0, g, m] * states[m] + value
                total = total + lam[1, g, m] * state
                after.append(state)
            ys[k, g, r] = total
            return tuple(after)

        zero = jnp.zeros((segs, lanes), jnp.float32)
        ends = lax.fori_loop(0, steps, step, (zero,) * modes, unroll=2)
        for m in range(modes):
            scan = ends[m]
            for n in range(3):
                scan = scan + jnp.where(
                    sub >= 1 << n, pw[n, g, m] * pltpu.roll(scan, 1 << n, 0), 0.0
                )
            carry = carry_ref[g, m]
            inits[k, g, m] = (
                jnp.where(sub == 0, 0.0, pltpu.roll(scan, 1, 0)) + pw[4, g, m] * carry
            )
            carry_ref[g, m] = fill(scan[segs - 1 : segs]) + pw[3, g, m] * carry


def finish_part(groups, modes, k, incoming, lam, pw, ys, inits, gs, outs):
    for g in range(groups):
        starts = []
        for m in range(modes):
            start = incoming[g, m]
            starts.append(lam[1, g, m] * (inits[k, g, m] + pw[4, g, m] * start))
            incoming[g, m] = pw[3, g, m] * start

        def step(r, states):
            total = ys[k, g, r]
            after = []
            for m in range(modes):
                state = lam[0, g, m] * states[m]
                total = total + state
                after.append(state)
            outs[g, pl.ds(r, segs, stride=steps), :] = gate_at(gs, groups, g, 0, r) * total
            return tuple(after)

        lax.fori_loop(0, steps, step, tuple(starts), unroll=2)


def load_gates(k, gates, gs):
    rows = chunk * 4
    gs[...] = gates[pl.ds(pl.multiple_of(k * rows, rows), rows), :].astype(jnp.float32)


def gate_at(gs, groups, g, which, r):
    return gs[pl.ds((r * groups + g) * 2 + which, segs, stride=steps * groups * 2), :]


MESH = pl.DeviceIdType.MESH
kinds = 10
waits = 8
halo_rows = taps + 16
unit = 128
part_rows = 24


def place_of(owner):
    return lax.rem(owner, 2) * 8 + lax.rem(owner // 2, 2) * 4 + owner // 4


class Mover:
    def __init__(self, units, resid_ref, own_rows, rows_ref, send_sem, recv_sem, own_sem):
        self.units = units
        self.resid, self.own_rows, self.rows = resid_ref, own_rows, rows_ref
        self.send_sem, self.recv_sem, self.own_sem = send_sem, recv_sem, own_sem
        me = lax.axis_index("chan")
        core, pair, x = lax.rem(me, 2), lax.rem(me // 2, 2), me // 4
        right, left, far = lax.rem(x + 1, 4), lax.rem(x + 3, 4), lax.rem(x + 2, 4)
        other = 1 - pair

        def block(x, y):
            return core * 8 + y * 4 + x

        def device(x, y):
            return x * 4 + y * 2 + core

        self.here = block(x, pair)
        whole, first, second = (0, unit), (0, unit // 2), (unit // 2, unit // 2)
        east, west, across = device(right, pair), device(left, pair), device(x, other)
        twin = me + 1 - 2 * core
        self.table = (
            (east, block(x, pair), whole, 1, 0),
            (west, block(x, pair), whole, 1, 1),
            (across, block(x, pair), whole, 1, 2),
            (east, block(left, pair), first, 1, 3),
            (west, block(right, pair), second, 1, 3),
            (east, block(x, other), whole, 1, 4),
            (west, block(x, other), whole, 1, 5),
            (across, block(far, pair), whole, 1, 6),
            (twin, block(0, pair), whole, 4, 7),
            (twin, block(0, other), whole, 4, 7),
        )
        self.landing = (
            (block(left, pair), 1),
            (block(right, pair), 1),
            (block(x, other), 1),
            (block(far, pair), 1),
            (block(left, other), 1),
            (block(right, other), 1),
            (block(far, other), 1),
            ((1 - core) * 8, 8),
        )
        self.twin = twin

    def token_rows(self, q):
        first = lax.rem(q + self.units - chunk // unit, self.units)
        return pl.ds(pl.multiple_of(first * unit, unit), unit)

    def place(self, q, begin, count, owner, blocks):
        rows = pl.ds(pl.multiple_of(lax.rem(q, chunk // unit) * unit + begin, count), count)
        cols = pl.ds(pl.multiple_of(owner * 256, 256), blocks * 256)
        return self.rows.at[q // (chunk // unit), rows, cols]

    def remote(self, source, target_ref, kind, q, wait, target):
        return pltpu.make_async_remote_copy(
            src_ref=source,
            dst_ref=target_ref,
            send_sem=self.send_sem.at[kind],
            recv_sem=self.recv_sem.at[q, wait],
            device_id={"chan": target},
            device_id_type=MESH,
        )

    def start(self, q, *which):
        for kind in which:
            target, sent, (begin, count), blocks, wait = self.table[kind]
            place = self.place(q, begin, count, sent, blocks)
            source = self.resid.at[self.token_rows(q), :] if kind < 3 else place
            self.remote(source, place, kind, q, wait, target).start()

    def sent(self):
        for kind in range(kinds):
            _, _, (_, count), blocks, _ = self.table[kind]
            if blocks == 1:
                whole = self.own_rows.at[pl.ds(0, self.units * count), :]
            else:
                whole = self.rows.at[:, :, pl.ds(0, blocks * 256)]
            self.remote(whole, whole, kind, 0, 0, self.twin).wait_send()

    def arrived(self, q, *which):
        for wait in which:
            owner, blocks = self.landing[wait]
            place = self.place(q, 0, unit, owner, blocks)
            self.remote(place, place, 0, q, wait, self.twin).wait_recv()

    def own(self, q):
        return pltpu.make_async_copy(
            self.resid.at[self.token_rows(q), :],
            self.place(q, 0, unit, self.here, 1),
            self.own_sem.at[q],
        )

    def stage_1(self, q):
        self.start(q, 0, 1, 2)
        self.own(q).start()

    def stage_2(self, q):
        self.arrived(q, 2)
        self.start(q, 5, 6)
        self.arrived(q, 0)
        self.start(q, 3)
        self.arrived(q, 1)
        self.start(q, 4)

    def stage_3(self, q):
        self.own(q).wait()
        self.arrived(q, 3)
        self.start(q, 7, 8)

    def stage_4(self, q):
        self.arrived(q, 4, 5, 6)
        self.start(q, 9)

    def stage_5(self, q):
        self.arrived(q, 7)

    def tick(self, t):
        stages = ((4, self.stage_3), (6, self.stage_2), (8, self.stage_1), (3, self.stage_4))
        for lead, stage in stages:
            if isinstance(t, int):
                if 0 <= t + lead < self.units:
                    stage(t + lead)
            else:
                pl.when(t + lead < self.units)(functools.partial(stage, t + lead))


def scale_weights(groups, peers, parts, wts):
    def body(j, c):
        for h in range(2):
            row = parts[j, 16 + h : 17 + h, :]
            column = jnp.transpose(jnp.broadcast_to(row, (lanes, lanes)))
            rows = pl.ds(pl.multiple_of(j * 256 + h * lanes, lanes), lanes)
            for s in range(3):
                for g in range(groups):
                    value = wts[s, rows, lane_tile(g)].astype(jnp.float32)
                    wts[s, rows, lane_tile(g)] = (value * column).astype(jnp.bfloat16)
        return c

    lax.fori_loop(0, peers, body, 0)


def square_rows(tokens, own_rows, parts, me):
    def body(i, c):
        value = own_rows[pl.ds(pl.multiple_of(i * lanes, lanes), lanes), :].astype(jnp.float32)
        total = jnp.zeros((lanes, lanes), jnp.float32)
        for g in range(value.shape[1] // lanes):
            total = total + value[:, lane_tile(g)] * value[:, lane_tile(g)]
        parts[me, pl.ds(i, 1), :] = jnp.sum(jnp.transpose(total), axis=0, keepdims=True)
        return c

    lax.fori_loop(0, tokens // lanes, body, 0)


def project(groups, q, first, rows_ref, wts, scales, pj):
    columns_of = [
        jnp.transpose(jnp.broadcast_to(scales[pl.ds(first + h, 1), :], (lanes, lanes)))
        for h in range(chunk // lanes)
    ]
    for s in range(3):
        value = jnp.dot(rows_ref[q], wts[s], preferred_element_type=jnp.float32)
        for g in range(groups):
            for h, scale in enumerate(columns_of):
                piece = value[lane_tile(h), lane_tile(g)] * scale
                pj[s * groups + g, lane_tile(h), :] = piece.astype(jnp.bfloat16).astype(jnp.float32)


def fused_kernel(
    groups, modes, chunks, sides, peers,
    resid_ref, weight_hbm, gates_hbm, gain_ref, sf_ref, mr_ref, decay_ref, residue_ref, skip_ref,
    out_ref,
    rows_ref, wts, gates, own_rows, parts, scales, pj, pj_last, halo_out, halo_in, states, outs,
    tail, sfb, qs, pe, fb, gs, ls, lam, skb, pw, carry_ref, incoming, ys, inits,
    send_sem, recv_sem, own_sem, gain_send, gain_recv, state_send, state_recv, halo_sem, weight_sem, own_load_sem, gates_sem,
):
    me, part = lax.axis_index("chan"), lax.axis_index("seq")
    own_load = pltpu.make_async_copy(resid_ref, own_rows, own_load_sem)
    own_load.start()
    load = pltpu.make_async_copy(weight_hbm, wts, weight_sem)
    for p in range(sides):
        owner = (p % 4) * 4 + (p % 8 // 4) * 2 + p // 8
        pltpu.make_async_copy(
            weight_hbm.at[:, owner * 256 : (owner + 1) * 256, :],
            wts.at[:, p * 256 : (p + 1) * 256, :],
            weight_sem,
        ).start()
    gates_load = pltpu.make_async_copy(gates_hbm, gates, gates_sem)
    gates_load.start()

    barrier = pltpu.get_barrier_semaphore()
    for o in range(1, sides):
        pl.semaphore_signal(barrier, inc=1, device_id={"chan": lax.rem(me + o, sides)}, device_id_type=MESH)
    for o in range(1, peers):
        pl.semaphore_signal(barrier, inc=1, device_id={"seq": lax.rem(part + o, peers)}, device_id_type=MESH)
    pl.semaphore_wait(barrier, sides + peers - 2)

    units = chunks * chunk // unit
    mover = Mover(units, resid_ref, own_rows, rows_ref, send_sem, recv_sem, own_sem)
    mover.tick(-8)
    mover.tick(-7)

    gain = gain_ref[...].reshape(1, 256).astype(jnp.float32)
    parts[mover.here, 16:17, :] = gain[:, lane_tile(0)]
    parts[mover.here, 17:18, :] = gain[:, lane_tile(1)]
    own_load.wait()
    square_rows(chunks * chunk, own_rows, parts, mover.here)
    mover.tick(-6)
    skip = skip_ref[...].reshape(1, 256)
    set_constants(groups, modes, sf_ref, mr_ref, decay_ref, residue_ref, skip, sfb, fb, lam, skb, pw)

    def part_copy(o):
        return pltpu.make_async_remote_copy(
            src_ref=parts.at[mover.here], dst_ref=parts.at[mover.here],
            send_sem=gain_send.at[o], recv_sem=gain_recv.at[o],
            device_id={"chan": lax.rem(me + o, sides)}, device_id_type=MESH,
        )

    for o in range(1, sides):
        part_copy(o).start()
    mover.tick(-5)
    carry_ref[...] = jnp.zeros_like(carry_ref)
    tail[...] = jnp.zeros_like(tail)
    pe[...] = jnp.zeros_like(pe)
    load.wait()
    mover.tick(-4)
    for o in range(1, sides):
        source = lax.rem(me + sides - o, sides)
        pltpu.make_async_remote_copy(
            src_ref=parts.at[place_of(source)], dst_ref=parts.at[place_of(source)],
            send_sem=gain_send.at[o], recv_sem=gain_recv.at[o],
            device_id={"chan": source}, device_id_type=MESH,
        ).wait_recv()
    squares = parts[0, 0:16, :]
    for p in range(1, sides):
        squares = squares + parts[p, 0:16, :]
    scales[...] = lax.rsqrt(squares / (sides * 256) + norm_epsilon)
    scale_weights(groups, sides, parts, wts)
    gates_load.wait()
    mover.tick(-3)
    mover.tick(-2)

    def halo_copy():
        return pltpu.make_async_remote_copy(
            src_ref=halo_out, dst_ref=halo_in,
            send_sem=halo_sem.at[0], recv_sem=halo_sem.at[1],
            device_id={"seq": lax.rem(part + 1, peers)}, device_id_type=MESH,
        )

    def body(q, c):
        @pl.when(q < chunks)
        def _():
            for h in range(chunk // unit):
                mover.stage_5(q * (chunk // unit) + h)

        mover.tick(2 * q - 1)

        @pl.when(q < chunks)
        def _():
            first = lax.rem(q + chunks - 1, chunks) * (chunk // lanes)
            project(groups, q, first, rows_ref, wts, scales, pj)

        @pl.when(q == 0)
        def _():
            for n in range(3 * groups):
                pj_last[n] = pj[n]
                halo_out[:, lane_tile(n)] = pj[n, chunk - halo_rows :, :].astype(jnp.bfloat16)
            halo_copy().start()

        @pl.when(q == 1)
        def _():
            halo_copy().wait()
            seen = jnp.where(part > 0, 1.0, 0.0)
            for n in range(3 * groups):
                outs[n] = jnp.zeros((chunk, lanes), jnp.float32)
                outs[n, chunk - halo_rows :, :] = halo_in[:, lane_tile(n)].astype(jnp.float32) * seen
            short_part(groups, outs, tail, sfb, qs, pe)

        @pl.when(q == chunks)
        def _():
            pj[...] = pj_last[...]

        @pl.when(q > 0)
        def _():
            short_part(groups, pj, tail, sfb, qs, pe)

        mover.tick(2 * q)

        @pl.when(q > 0)
        def _():
            k = q - 1
            load_gates(k, gates, gs)
            medium_part(groups, pe, fb, qs, gs, ls)
            long_part(groups, modes, k, ls, lam, skb, pw, carry_ref, ys, inits)

        return c

    lax.fori_loop(0, chunks + 1, body, 0)

    for g in range(groups):
        for m in range(modes):
            states[0, g, m : m + 1, :] = carry_ref[g, m, 0:1, :]

    def state_copy(o):
        return pltpu.make_async_remote_copy(
            src_ref=states.at[0], dst_ref=states.at[o],
            send_sem=state_send.at[o], recv_sem=state_recv.at[o],
            device_id={"seq": lax.rem(part + o, peers)}, device_id_type=MESH,
        )

    for o in range(1, peers):
        state_copy(o).start()

    mover.sent()
    for o in range(1, sides):
        part_copy(o).wait_send()
    for o in range(1, peers):
        state_copy(o).wait()
    for g in range(groups):
        total = jnp.zeros((modes, lanes), jnp.float32)
        d = decay_ref[:, lane_tile(g)]
        for o in range(1, peers):
            weight = jnp.exp(d * (-1.0 * chunk * chunks * (o - 1)))
            total = total + jnp.where(part >= o, weight, 0.0) * states[o, g]
        for m in range(modes):
            incoming[g, m] = fill(total[m : m + 1])

    def finish(k, c):
        load_gates(k, gates, gs)
        finish_part(groups, modes, k, incoming, lam, pw, ys, inits, gs, outs)
        rows = pl.ds(pl.multiple_of(k * chunk, chunk), chunk)
        for g in range(groups):
            out_ref[rows, lane_tile(g)] = outs[g].astype(jnp.bfloat16)
        return c

    lax.fori_loop(0, chunks, finish, 0)


def in_vmem(n):
    return [pl.BlockSpec(memory_space=pltpu.VMEM)] * n


def vregs(*lead):
    return pltpu.VMEM(lead + (segs, lanes), jnp.float32)


def fused_call(resid, weight, gates, gain, short_filter, mr_filter, decays, residue, skip):
    length, width = resid.shape
    modes = decays.shape[0]
    groups, chunks = width // lanes, length // chunk
    sides, peers = lax.axis_size("chan"), lax.axis_size("seq")
    units = length // unit
    f32, bf16 = jnp.float32, jnp.bfloat16
    dma = pltpu.SemaphoreType.DMA
    anywhere = pl.BlockSpec(memory_space=pl.ANY)
    vmem = pl.BlockSpec(memory_space=pltpu.VMEM)
    return pl.pallas_call(
        functools.partial(fused_kernel, groups, modes, chunks, sides, peers),
        out_shape=jax.ShapeDtypeStruct((length, width), bf16),
        in_specs=[anywhere] * 3 + [vmem] * 6,
        out_specs=vmem,
        scratch_shapes=[
            pltpu.VMEM((chunks, chunk, sides * width), bf16),
            pltpu.VMEM((3, sides * width, width), bf16),
            pltpu.VMEM(gates.shape, bf16),
            pltpu.VMEM((length, width), bf16),
            pltpu.VMEM((sides, part_rows, lanes), f32),
            pltpu.VMEM((length // lanes, lanes), f32),
            pltpu.VMEM((3 * groups, chunk, lanes), f32),
            pltpu.VMEM((3 * groups, chunk, lanes), f32),
            pltpu.VMEM((halo_rows, 3 * width), bf16),
            pltpu.VMEM((halo_rows, 3 * width), bf16),
            pltpu.VMEM((peers, groups, modes, lanes), f32),
            pltpu.VMEM((3 * groups, chunk, lanes), f32),
            vregs(3 * groups, 2),
            vregs(9 * groups),
            vregs(groups, steps),
            vregs(groups, taps + steps),
            vregs(groups, taps),
            pltpu.VMEM((chunk * 2 * groups, lanes), f32),
            vregs(groups, steps),
            vregs(2, groups, modes),
            vregs(groups),
            vregs(5, groups, modes),
            vregs(groups, modes),
            vregs(groups, modes),
            vregs(chunks, groups, steps),
            vregs(chunks, groups, modes),
            dma((kinds,)),
            dma((units, waits)),
            dma((units,)),
            dma((sides,)),
            dma((sides,)),
            dma((peers,)),
            dma((peers,)),
            dma((2,)),
            dma,
            dma,
            dma,
        ],
        compiler_params=pltpu.CompilerParams(
            vmem_limit_bytes=60 << 20, collective_id=0, has_side_effects=True
        ),
    )(resid, weight, gates, gain, short_filter, mr_filter, decays, residue, skip)


def on_device(
    resid, norm_gain, feat_weight, short_filter, mr_filter, gates_lr, decay_rate, residue, skip_gain
):
    tokens, two, width = gates_lr.shape
    gates = gates_lr.reshape(tokens, two, width // lanes, lanes).transpose(0, 2, 1, 3)
    return fused_call(
        resid,
        jnp.transpose(feat_weight, (1, 0, 2)),
        gates.reshape(tokens * two * (width // lanes), lanes),
        norm_gain,
        short_filter,
        mr_filter,
        decay_rate,
        residue,
        skip_gain,
    )


def solution(mesh):
    in_specs = (
        P("seq", "chan"),
        P("chan"),
        P(None, None, "chan"),
        P(None, None, "chan"),
        P(None, "chan"),
        P("seq", None, "chan"),
        P(None, "chan"),
        P(None, "chan"),
        P("chan"),
    )
    return jax.shard_map(
        on_device, mesh=mesh, in_specs=in_specs, out_specs=P("seq", "chan"), check_vma=False
    )
```

```python
import functools

import jax
import jax.numpy as jnp
from jax import lax
from jax.experimental import pallas as pl
from jax.experimental.pallas import tpu as pltpu
from jax.sharding import PartitionSpec as P

norm_epsilon = 1e-05
lanes = 128
segs = 8
steps = 32
chunk = segs * steps
taps = 128
back = taps // steps
phases = 4
short_steps = steps // phases
short_taps = taps // phases
sums = ((0, 2), (1, 3), (0, 1), (2, 3), (4, 5))
parts_of = phases + len(sums)
halves = ((0, 2, 4), (1, 3, 5), (6, 7, 8))
early = (1, 2, 3, 5, 7)


def sublane():
    return lax.broadcasted_iota(jnp.int32, (segs, lanes), 0)


def fill(row):
    return jnp.broadcast_to(row, (segs, lanes))


def lane_tile(i):
    return slice(i * lanes, (i + 1) * lanes)


def modal_weights(decay, residue):
    x = decay * 2.0
    small = x * (1.0 - x / 2.0 * (1.0 - x / 3.0 * (1.0 - x / 4.0 * (1.0 - x / 5.0 * (1.0 - x / 6.0)))))
    return residue * jnp.sqrt(jnp.where(x < 0.125, small, 1.0 - jnp.exp(-x)))


def set_constants(groups, modes, sf_ref, mr_ref, decay_ref, residue_ref, skip, sfb, fb, lam, skb, pw):
    for g in range(groups):
        cols = lane_tile(g)
        for s in range(3):
            for j in range(3):
                sfb[(s * groups + g) * 3 + j] = fill(sf_ref[j, s : s + 1, cols])
        skb[g] = fill(skip[:, cols])

        def taps_at(t, carry):
            rows = mr_ref[pl.ds(pl.multiple_of(t * 16, 16), 16), cols].astype(jnp.float32)
            for j in range(16 // phases):
                values = [fill(rows[phases * j + i : phases * j + i + 1]) for i in range(phases)]
                for a, b in sums:
                    values.append(values[a] + values[b])
                for n, value in enumerate(values):
                    fb[g, n, t * (16 // phases) + j] = value
            return carry

        lax.fori_loop(0, taps // 16, taps_at, 0)
        at = sublane().astype(jnp.float32) * float(steps)
        modal = modal_weights(decay_ref[:, cols], residue_ref[:, cols])
        for m in range(modes):
            d = fill(decay_ref[m : m + 1, cols])
            lam[0, g, m] = jnp.exp(-d)
            lam[1, g, m] = fill(modal[m : m + 1])
            pw[0, g, m] = jnp.exp(d * (-1.0 * steps))
            pw[1, g, m] = jnp.exp(d * (-2.0 * steps))
            pw[2, g, m] = jnp.exp(d * (-4.0 * steps))
            pw[3, g, m] = jnp.exp(d * (-8.0 * steps))
            pw[4, g, m] = jnp.exp(-d * at)


def strided(ref, lead, r):
    return ref[lead, pl.ds(r, segs, stride=steps), :]


def short_part(groups, pj, tail, sfb, qs, ps):
    sub = sublane()
    for g in range(groups):
        names = [s * groups + g for s in range(3)]
        old = []
        for n in names:
            last = strided(pj, n, steps - 1)
            before = strided(pj, n, steps - 2)
            turned = (pltpu.roll(last, 1, 0), pltpu.roll(before, 1, 0))
            old.append(
                (
                    jnp.where(sub == 0, tail[n, 0], turned[0]),
                    jnp.where(sub == 0, tail[n, 1], turned[1]),
                )
            )
            tail[n, 0] = turned[0]
            tail[n, 1] = turned[1]

        def step(n, carry):
            products = []
            for i in range(phases):
                r = n * phases + i
                after, featured = [], []
                for name, (one, two) in zip(names, carry):
                    now = strided(pj, name, r)
                    featured.append(
                        sfb[name * 3] * now + sfb[name * 3 + 1] * one + sfb[name * 3 + 2] * two
                    )
                    after.append((now, one))
                carry = tuple(after)
                products.append((featured[1] * featured[2]).astype(jnp.bfloat16).astype(jnp.float32))
                qs[g, r] = featured[0]
            past = [ps[g, i, short_taps + n] for i in range(phases)]
            for shift in range(back + 1):
                values = products
                if shift > 0:
                    values = [
                        pltpu.roll(jnp.where(sub >= segs - shift, old, new), shift, 0)
                        for old, new in zip(past, products)
                    ]
                values = list(values)
                for x, y in sums:
                    values.append(values[x] + values[y])
                for i, value in enumerate(values):
                    ps[g, i, short_taps - shift * short_steps + n] = value
            return carry

        lax.fori_loop(0, short_steps, step, tuple(old))


def medium_part(groups, ps, fb, qs, gs, ls, yb):
    for g in range(groups):
        for n in range(parts_of):
            begin = -1 if n in early else 0
            totals = {}
            for j in range(short_taps):
                tap = fb[g, n, j]
                for i in range(begin, short_steps):
                    term = tap * ps[g, n, short_taps + i - j]
                    totals[i] = term if j == 0 else totals[i] + term
            for i in range(begin, short_steps):
                yb[n, i + 1] = totals[i]

        def half(which, i):
            even, odd, both = halves[which]
            n = i // 2
            if i % 2 == 0:
                return yb[even, n + 1] + yb[odd, n]
            return yb[both, n + 1] - yb[even, n + 1] - yb[odd, n + 1]

        before = half(1, -1)
        for m in range(steps // 2):
            evens, odds, both = half(0, m), half(1, m), half(2, m)
            for r, medium in ((2 * m, evens + before), (2 * m + 1, both - evens - odds)):
                mixed = (qs[g, r] * medium).astype(jnp.bfloat16).astype(jnp.float32)
                gate = gate_at(gs, groups, g, 1, r)
                ls[g, r] = (gate * mixed).astype(jnp.bfloat16).astype(jnp.float32)
            before = odds


def long_part(groups, modes, k, ls, lam, skb, pw, carry_ref, ys, inits):
    sub = sublane()
    for g in range(groups):

        def step(r, states):
            value = ls[g, r]
            total = skb[g] * value
            after = []
            for m in range(modes):
                state = lam[0, g, m] * states[m] + value
                total = total + lam[1, g, m] * state
                after.append(state)
            ys[k, g, r] = total
            return tuple(after)

        zero = jnp.zeros((segs, lanes), jnp.float32)
        ends = lax.fori_loop(0, steps, step, (zero,) * modes, unroll=2)
        for m in range(modes):
            scan = ends[m]
            for n in range(3):
                scan = scan + jnp.where(
                    sub >= 1 << n, pw[n, g, m] * pltpu.roll(scan, 1 << n, 0), 0.0
                )
            carry = carry_ref[g, m]
            inits[k, g, m] = (
                jnp.where(sub == 0, 0.0, pltpu.roll(scan, 1, 0)) + pw[4, g, m] * carry
            )
            carry_ref[g, m] = fill(scan[segs - 1 : segs]) + pw[3, g, m] * carry


def finish_part(groups, modes, k, incoming, lam, pw, ys, inits, gs, outs):
    for g in range(groups):
        starts = []
        for m in range(modes):
            start = incoming[g, m]
            starts.append(lam[1, g, m] * (inits[k, g, m] + pw[4, g, m] * start))
            incoming[g, m] = pw[3, g, m] * start

        def step(r, states):
            total = ys[k, g, r]
            after = []
            for m in range(modes):
                state = lam[0, g, m] * states[m]
                total = total + state
                after.append(state)
            outs[g, pl.ds(pl.multiple_of(r * segs, segs), segs), :] = gate_at(gs, groups, g, 0, r) * total
            return tuple(after)

        lax.fori_loop(0, steps, step, tuple(starts), unroll=2)


def load_gates(k, gates, gs):
    rows = chunk * 4
    gs[...] = gates[pl.ds(pl.multiple_of(k * rows, rows), rows), :].astype(jnp.float32)


def gate_at(gs, groups, g, which, r):
    return gs[pl.ds((r * groups + g) * 2 + which, segs, stride=steps * groups * 2), :]


MESH = pl.DeviceIdType.MESH
kinds = 10
waits = 8
unit = 128
part_rows = 24


def place_of(owner):
    return lax.rem(owner, 2) * 8 + lax.rem(owner // 2, 2) * 4 + owner // 4


class Mover:
    def __init__(self, units, resid_ref, own_rows, rows_ref, send_sem, recv_sem, own_sem):
        self.units = units
        self.resid, self.own_rows, self.rows = resid_ref, own_rows, rows_ref
        self.send_sem, self.recv_sem, self.own_sem = send_sem, recv_sem, own_sem
        me = lax.axis_index("chan")
        core, pair, x = lax.rem(me, 2), lax.rem(me // 2, 2), me // 4
        right, left, far = lax.rem(x + 1, 4), lax.rem(x + 3, 4), lax.rem(x + 2, 4)
        other = 1 - pair

        def block(x, y):
            return core * 8 + y * 4 + x

        def device(x, y):
            return x * 4 + y * 2 + core

        self.here = block(x, pair)
        whole, first, second = (0, unit), (0, unit // 2), (unit // 2, unit // 2)
        east, west, across = device(right, pair), device(left, pair), device(x, other)
        twin = me + 1 - 2 * core
        self.table = (
            (east, block(x, pair), whole, 1, 0),
            (west, block(x, pair), whole, 1, 1),
            (across, block(x, pair), whole, 1, 2),
            (east, block(left, pair), first, 1, 3),
            (west, block(right, pair), second, 1, 3),
            (east, block(x, other), whole, 1, 4),
            (west, block(x, other), whole, 1, 5),
            (across, block(far, pair), whole, 1, 6),
            (twin, block(0, pair), whole, 4, 7),
            (twin, block(0, other), whole, 4, 7),
        )
        self.landing = (
            (block(left, pair), 1),
            (block(right, pair), 1),
            (block(x, other), 1),
            (block(far, pair), 1),
            (block(left, other), 1),
            (block(right, other), 1),
            (block(far, other), 1),
            ((1 - core) * 8, 8),
        )
        self.twin = twin

    def token_rows(self, q):
        first = lax.rem(q + self.units - chunk // unit, self.units)
        return pl.ds(pl.multiple_of(first * unit, unit), unit)

    def place(self, q, begin, count, owner, blocks):
        rows = pl.ds(pl.multiple_of(lax.rem(q, chunk // unit) * unit + begin, count), count)
        cols = pl.ds(pl.multiple_of(owner * 256, 256), blocks * 256)
        return self.rows.at[q // (chunk // unit), rows, cols]

    def remote(self, source, target_ref, kind, q, wait, target):
        return pltpu.make_async_remote_copy(
            src_ref=source,
            dst_ref=target_ref,
            send_sem=self.send_sem.at[kind],
            recv_sem=self.recv_sem.at[q, wait],
            device_id={"chan": target},
            device_id_type=MESH,
        )

    def start(self, q, *which):
        for kind in which:
            target, sent, (begin, count), blocks, wait = self.table[kind]
            place = self.place(q, begin, count, sent, blocks)
            source = self.resid.at[self.token_rows(q), :] if kind < 3 else place
            self.remote(source, place, kind, q, wait, target).start()

    def sent(self):
        for kind in range(kinds):
            _, _, (_, count), blocks, _ = self.table[kind]
            if blocks == 1:
                whole = self.own_rows.at[pl.ds(0, self.units * count), :]
            else:
                whole = self.rows.at[:, :, pl.ds(0, blocks * 256)]
            self.remote(whole, whole, kind, 0, 0, self.twin).wait_send()

    def arrived(self, q, *which):
        for wait in which:
            owner, blocks = self.landing[wait]
            place = self.place(q, 0, unit, owner, blocks)
            self.remote(place, place, 0, q, wait, self.twin).wait_recv()

    def own(self, q):
        return pltpu.make_async_copy(
            self.resid.at[self.token_rows(q), :],
            self.place(q, 0, unit, self.here, 1),
            self.own_sem.at[q],
        )

    def stage_1(self, q):
        self.start(q, 0, 1, 2)
        self.own(q).start()

    def stage_2(self, q):
        self.arrived(q, 2)
        self.start(q, 5, 6)
        self.arrived(q, 0)
        self.start(q, 3)
        self.arrived(q, 1)
        self.start(q, 4)

    def stage_3(self, q):
        self.own(q).wait()
        self.arrived(q, 3)
        self.start(q, 7, 8)

    def stage_4(self, q):
        self.arrived(q, 4, 5, 6)
        self.start(q, 9)

    def stage_5(self, q):
        self.arrived(q, 7)

    def tick(self, t):
        stages = ((4, self.stage_3), (6, self.stage_2), (8, self.stage_1), (3, self.stage_4))
        for lead, stage in stages:
            if isinstance(t, int):
                if 0 <= t + lead < self.units:
                    stage(t + lead)
            else:
                pl.when(t + lead < self.units)(functools.partial(stage, t + lead))


def scale_weights(groups, peers, parts, wts):
    def body(j, c):
        for h in range(2):
            row = parts[j, 16 + h : 17 + h, :]
            column = jnp.transpose(jnp.broadcast_to(row, (lanes, lanes)))
            rows = pl.ds(pl.multiple_of(j * 256 + h * lanes, lanes), lanes)
            for s in range(3):
                for g in range(groups):
                    value = wts[s, rows, lane_tile(g)].astype(jnp.float32)
                    wts[s, rows, lane_tile(g)] = (value * column).astype(jnp.bfloat16)
        return c

    lax.fori_loop(0, peers, body, 0)


def square_rows(tokens, own_rows, parts, me):
    def body(i, c):
        value = own_rows[pl.ds(pl.multiple_of(i * lanes, lanes), lanes), :].astype(jnp.float32)
        total = jnp.zeros((lanes, lanes), jnp.float32)
        for g in range(value.shape[1] // lanes):
            total = total + value[:, lane_tile(g)] * value[:, lane_tile(g)]
        parts[me, pl.ds(i, 1), :] = jnp.sum(jnp.transpose(total), axis=0, keepdims=True)
        return c

    lax.fori_loop(0, tokens // lanes, body, 0)


def project(groups, q, first, rows_ref, wts, scales, pj):
    columns_of = [
        jnp.transpose(jnp.broadcast_to(scales[pl.ds(first + h, 1), :], (lanes, lanes)))
        for h in range(chunk // lanes)
    ]
    for s in range(3):
        value = jnp.dot(rows_ref[q], wts[s], preferred_element_type=jnp.float32)
        for g in range(groups):
            for h, scale in enumerate(columns_of):
                piece = value[lane_tile(h), lane_tile(g)] * scale
                pj[s * groups + g, lane_tile(h), :] = piece.astype(jnp.bfloat16).astype(jnp.float32)


def fused_kernel(
    groups, modes, chunks, sides, peers,
    resid_ref, weight_hbm, gates_hbm, gain_ref, sf_ref, mr_ref, decay_ref, residue_ref, skip_ref,
    out_ref,
    rows_ref, wts, gates, own_rows, parts, scales, pj, pj_last, halo_in, tail_in, states, outs,
    tail, sfb, qs, ps, yb, fb, gs, ls, lam, skb, pw, carry_ref, incoming, ys, inits,
    send_sem, recv_sem, own_sem, gain_send, gain_recv, state_send, state_recv, halo_sem, weight_sem, own_load_sem, gates_sem,
):
    me, part = lax.axis_index("chan"), lax.axis_index("seq")
    own_load = pltpu.make_async_copy(resid_ref, own_rows, own_load_sem)
    own_load.start()
    load = pltpu.make_async_copy(weight_hbm, wts, weight_sem)
    for p in range(sides):
        owner = (p % 4) * 4 + (p % 8 // 4) * 2 + p // 8
        pltpu.make_async_copy(
            weight_hbm.at[:, owner * 256 : (owner + 1) * 256, :],
            wts.at[:, p * 256 : (p + 1) * 256, :],
            weight_sem,
        ).start()
    gates_load = pltpu.make_async_copy(gates_hbm, gates, gates_sem)
    gates_load.start()

    barrier = pltpu.get_barrier_semaphore()
    for o in range(1, sides):
        pl.semaphore_signal(barrier, inc=1, device_id={"chan": lax.rem(me + o, sides)}, device_id_type=MESH)
    for o in range(1, peers):
        pl.semaphore_signal(barrier, inc=1, device_id={"seq": lax.rem(part + o, peers)}, device_id_type=MESH)
    pl.semaphore_wait(barrier, sides + peers - 2)

    units = chunks * chunk // unit
    mover = Mover(units, resid_ref, own_rows, rows_ref, send_sem, recv_sem, own_sem)
    mover.tick(-8)
    mover.tick(-7)

    gain = gain_ref[...].reshape(1, 256).astype(jnp.float32)
    parts[mover.here, 16:17, :] = gain[:, lane_tile(0)]
    parts[mover.here, 17:18, :] = gain[:, lane_tile(1)]
    own_load.wait()
    square_rows(chunks * chunk, own_rows, parts, mover.here)
    mover.tick(-6)
    skip = skip_ref[...].reshape(1, 256)
    set_constants(groups, modes, sf_ref, mr_ref, decay_ref, residue_ref, skip, sfb, fb, lam, skb, pw)

    def part_copy(o):
        return pltpu.make_async_remote_copy(
            src_ref=parts.at[mover.here], dst_ref=parts.at[mover.here],
            send_sem=gain_send.at[o], recv_sem=gain_recv.at[o],
            device_id={"chan": lax.rem(me + o, sides)}, device_id_type=MESH,
        )

    for o in range(1, sides):
        part_copy(o).start()
    mover.tick(-5)
    carry_ref[...] = jnp.zeros_like(carry_ref)
    tail[...] = jnp.zeros_like(tail)
    ps[...] = jnp.zeros_like(ps)
    load.wait()
    mover.tick(-4)
    for o in range(1, sides):
        source = lax.rem(me + sides - o, sides)
        pltpu.make_async_remote_copy(
            src_ref=parts.at[place_of(source)], dst_ref=parts.at[place_of(source)],
            send_sem=gain_send.at[o], recv_sem=gain_recv.at[o],
            device_id={"chan": source}, device_id_type=MESH,
        ).wait_recv()
    squares = parts[0, 0:16, :]
    for p in range(1, sides):
        squares = squares + parts[p, 0:16, :]
    scales[...] = lax.rsqrt(squares / (sides * 256) + norm_epsilon)
    scale_weights(groups, sides, parts, wts)
    gates_load.wait()
    mover.tick(-3)
    mover.tick(-2)

    def halo_copies():
        sent = (
            (ps.at[:, pl.ds(0, phases), pl.ds(short_taps, short_steps), pl.ds(segs - back, back), :], halo_in),
            (tail.at[:, :, pl.ds(0, 1), :], tail_in),
        )
        return [
            pltpu.make_async_remote_copy(
                src_ref=source, dst_ref=target,
                send_sem=halo_sem.at[2 * n], recv_sem=halo_sem.at[2 * n + 1],
                device_id={"seq": lax.rem(part + 1, peers)}, device_id_type=MESH,
            )
            for n, (source, target) in enumerate(sent)
        ]

    def body(q, c):
        @pl.when(q < chunks)
        def _():
            for h in range(chunk // unit):
                mover.stage_5(q * (chunk // unit) + h)

        mover.tick(2 * q - 1)

        @pl.when(q < chunks)
        def _():
            first = lax.rem(q + chunks - 1, chunks) * (chunk // lanes)
            project(groups, q, first, rows_ref, wts, scales, pj)

        @pl.when(q == 0)
        def _():
            pj_last[...] = pj[...]
            short_part(groups, pj, tail, sfb, qs, ps)
            for copy in halo_copies():
                copy.start()

        @pl.when(q == 1)
        def _():
            for copy in halo_copies():
                copy.wait()
            seen = jnp.where(part > 0, 1.0, 0.0)
            for g in range(groups):
                for i in range(phases):
                    for n in range(short_steps):
                        ps[g, i, short_taps + n, segs - back :, :] = halo_in[g, i, n] * seen
            for n in range(3 * groups):
                for i in range(2):
                    tail[n, i, 0:1, :] = tail_in[n, i] * seen

        @pl.when(q == chunks)
        def _():
            pj[...] = pj_last[...]

        @pl.when(q > 0)
        def _():
            short_part(groups, pj, tail, sfb, qs, ps)

        mover.tick(2 * q)

        @pl.when(q > 0)
        def _():
            k = q - 1
            load_gates(k, gates, gs)
            medium_part(groups, ps, fb, qs, gs, ls, yb)
            long_part(groups, modes, k, ls, lam, skb, pw, carry_ref, ys, inits)

        return c

    lax.fori_loop(0, chunks + 1, body, 0)

    for g in range(groups):
        for m in range(modes):
            states[0, g, m : m + 1, :] = carry_ref[g, m, 0:1, :]

    def state_copy(o):
        return pltpu.make_async_remote_copy(
            src_ref=states.at[0], dst_ref=states.at[o],
            send_sem=state_send.at[o], recv_sem=state_recv.at[o],
            device_id={"seq": lax.rem(part + o, peers)}, device_id_type=MESH,
        )

    for o in range(1, peers):
        state_copy(o).start()

    mover.sent()
    for o in range(1, sides):
        part_copy(o).wait_send()
    for o in range(1, peers):
        state_copy(o).wait()
    for g in range(groups):
        total = jnp.zeros((modes, lanes), jnp.float32)
        d = decay_ref[:, lane_tile(g)]
        for o in range(1, peers):
            weight = jnp.exp(d * (-1.0 * chunk * chunks * (o - 1)))
            total = total + jnp.where(part >= o, weight, 0.0) * states[o, g]
        for m in range(modes):
            incoming[g, m] = fill(total[m : m + 1])

    def finish(k, c):
        load_gates(k, gates, gs)
        finish_part(groups, modes, k, incoming, lam, pw, ys, inits, gs, outs)
        for g in range(groups):
            for seg in range(segs):
                for r in range(0, steps, 16):
                    pieces = [
                        outs[g, pl.ds((r + half) * segs + seg, 8, stride=segs), :] for half in (0, 8)
                    ]
                    rows = pl.ds(pl.multiple_of(k * chunk + seg * steps + r, 16), 16)
                    out_ref[rows, lane_tile(g)] = jnp.concatenate(pieces, axis=0).astype(jnp.bfloat16)
        return c

    lax.fori_loop(0, chunks, finish, 0)


def in_vmem(n):
    return [pl.BlockSpec(memory_space=pltpu.VMEM)] * n


def vregs(*lead):
    return pltpu.VMEM(lead + (segs, lanes), jnp.float32)


def fused_call(resid, weight, gates, gain, short_filter, mr_filter, decays, residue, skip):
    length, width = resid.shape
    modes = decays.shape[0]
    groups, chunks = width // lanes, length // chunk
    sides, peers = lax.axis_size("chan"), lax.axis_size("seq")
    units = length // unit
    f32, bf16 = jnp.float32, jnp.bfloat16
    dma = pltpu.SemaphoreType.DMA
    anywhere = pl.BlockSpec(memory_space=pl.ANY)
    vmem = pl.BlockSpec(memory_space=pltpu.VMEM)
    return pl.pallas_call(
        functools.partial(fused_kernel, groups, modes, chunks, sides, peers),
        out_shape=jax.ShapeDtypeStruct((length, width), bf16),
        in_specs=[anywhere] * 3 + [vmem] * 6,
        out_specs=vmem,
        scratch_shapes=[
            pltpu.VMEM((chunks, chunk, sides * width), bf16),
            pltpu.VMEM((3, sides * width, width), bf16),
            pltpu.VMEM(gates.shape, bf16),
            pltpu.VMEM((length, width), bf16),
            pltpu.VMEM((sides, part_rows, lanes), f32),
            pltpu.VMEM((length // lanes, lanes), f32),
            pltpu.VMEM((3 * groups, chunk, lanes), f32),
            pltpu.VMEM((3 * groups, chunk, lanes), f32),
            pltpu.VMEM((groups, phases, short_steps, back, lanes), f32),
            pltpu.VMEM((3 * groups, 2, 1, lanes), f32),
            pltpu.VMEM((peers, groups, modes, lanes), f32),
            pltpu.VMEM((groups, chunk, lanes), f32),
            vregs(3 * groups, 2),
            vregs(9 * groups),
            vregs(groups, steps),
            vregs(groups, parts_of, short_taps + short_steps),
            vregs(parts_of, short_steps + 1),
            vregs(groups, parts_of, short_taps),
            pltpu.VMEM((chunk * 2 * groups, lanes), f32),
            vregs(groups, steps),
            vregs(2, groups, modes),
            vregs(groups),
            vregs(5, groups, modes),
            vregs(groups, modes),
            vregs(groups, modes),
            vregs(chunks, groups, steps),
            vregs(chunks, groups, modes),
            dma((kinds,)),
            dma((units, waits)),
            dma((units,)),
            dma((sides,)),
            dma((sides,)),
            dma((peers,)),
            dma((peers,)),
            dma((4,)),
            dma,
            dma,
            dma,
        ],
        compiler_params=pltpu.CompilerParams(
            vmem_limit_bytes=60 << 20, collective_id=0, has_side_effects=True
        ),
    )(resid, weight, gates, gain, short_filter, mr_filter, decays, residue, skip)


def on_device(
    resid, norm_gain, feat_weight, short_filter, mr_filter, gates_lr, decay_rate, residue, skip_gain
):
    tokens, two, width = gates_lr.shape
    gates = gates_lr.reshape(tokens, two, width // lanes, lanes).transpose(0, 2, 1, 3)
    return fused_call(
        resid,
        jnp.transpose(feat_weight, (1, 0, 2)),
        gates.reshape(tokens * two * (width // lanes), lanes),
        norm_gain,
        short_filter,
        mr_filter,
        decay_rate,
        residue,
        skip_gain,
    )


def solution(mesh):
    in_specs = (
        P("seq", "chan"),
        P("chan"),
        P(None, None, "chan"),
        P(None, None, "chan"),
        P(None, "chan"),
        P("seq", None, "chan"),
        P(None, "chan"),
        P(None, "chan"),
        P("chan"),
    )
    return jax.shard_map(
        on_device, mesh=mesh, in_specs=in_specs, out_specs=P("seq", "chan"), check_vma=False
    )
```

```python
import functools

import jax
import jax.numpy as jnp
from jax import lax
from jax.experimental import pallas as pl
from jax.experimental.pallas import tpu as pltpu
from jax.sharding import PartitionSpec as P

norm_epsilon = 1e-05
lanes = 128
segs = 8
steps = 32
chunk = segs * steps
taps = 128
back = taps // steps
phases = 4
short_steps = steps // phases
short_taps = taps // phases
sums = ((0, 2), (1, 3), (0, 1), (2, 3), (4, 5))
parts_of = phases + len(sums)
halves = ((0, 2, 4), (1, 3, 5), (6, 7, 8))
early = (1, 2, 3, 5, 7)


def sublane():
    return lax.broadcasted_iota(jnp.int32, (segs, lanes), 0)


def fill(row):
    return jnp.broadcast_to(row, (segs, lanes))


def lane_tile(i):
    return slice(i * lanes, (i + 1) * lanes)


def modal_weights(decay, residue):
    x = decay * 2.0
    small = x * (1.0 - x / 2.0 * (1.0 - x / 3.0 * (1.0 - x / 4.0 * (1.0 - x / 5.0 * (1.0 - x / 6.0)))))
    return residue * jnp.sqrt(jnp.where(x < 0.125, small, 1.0 - jnp.exp(-x)))


def set_constants(groups, modes, sf_ref, mr_ref, decay_ref, residue_ref, skip, sfb, fb, lam, skb, pw):
    for g in range(groups):
        cols = lane_tile(g)
        for s in range(3):
            for j in range(3):
                sfb[(s * groups + g) * 3 + j] = fill(sf_ref[j, s : s + 1, cols])
        skb[g] = fill(skip[:, cols])

        def taps_at(t, carry):
            rows = mr_ref[pl.ds(pl.multiple_of(t * 16, 16), 16), cols].astype(jnp.float32)
            for j in range(16 // phases):
                values = [fill(rows[phases * j + i : phases * j + i + 1]) for i in range(phases)]
                for a, b in sums:
                    values.append(values[a] + values[b])
                for n, value in enumerate(values):
                    fb[g, n, t * (16 // phases) + j] = value
            return carry

        lax.fori_loop(0, taps // 16, taps_at, 0)
        at = sublane().astype(jnp.float32) * float(steps)
        modal = modal_weights(decay_ref[:, cols], residue_ref[:, cols])
        for m in range(modes):
            d = fill(decay_ref[m : m + 1, cols])
            lam[0, g, m] = jnp.exp(-d)
            lam[1, g, m] = fill(modal[m : m + 1])
            pw[0, g, m] = jnp.exp(d * (-1.0 * steps))
            pw[1, g, m] = jnp.exp(d * (-2.0 * steps))
            pw[2, g, m] = jnp.exp(d * (-4.0 * steps))
            pw[3, g, m] = jnp.exp(d * (-8.0 * steps))
            pw[4, g, m] = jnp.exp(-d * at)


def strided(ref, lead, r):
    return ref[lead, pl.ds(r, segs, stride=steps), :]


def short_part(groups, pj, tail, sfb, qs, ps):
    sub = sublane()
    for g in range(groups):
        names = [s * groups + g for s in range(3)]
        old = []
        for n in names:
            last = strided(pj, n, steps - 1)
            before = strided(pj, n, steps - 2)
            turned = (pltpu.roll(last, 1, 0), pltpu.roll(before, 1, 0))
            old.append(
                (
                    jnp.where(sub == 0, tail[n, 0], turned[0]),
                    jnp.where(sub == 0, tail[n, 1], turned[1]),
                )
            )
            tail[n, 0] = turned[0]
            tail[n, 1] = turned[1]

        def step(n, carry):
            products = []
            for i in range(phases):
                r = n * phases + i
                after, featured = [], []
                for name, (one, two) in zip(names, carry):
                    now = strided(pj, name, r)
                    featured.append(
                        sfb[name * 3] * now + sfb[name * 3 + 1] * one + sfb[name * 3 + 2] * two
                    )
                    after.append((now, one))
                carry = tuple(after)
                products.append((featured[1] * featured[2]).astype(jnp.bfloat16).astype(jnp.float32))
                qs[g, r] = featured[0]
            past = [ps[g, i, short_taps + n] for i in range(phases)]
            for shift in range(back + 1):
                values = products
                if shift > 0:
                    values = [
                        pltpu.roll(jnp.where(sub >= segs - shift, old, new), shift, 0)
                        for old, new in zip(past, products)
                    ]
                values = list(values)
                for x, y in sums:
                    values.append(values[x] + values[y])
                for i, value in enumerate(values):
                    ps[g, i, short_taps - shift * short_steps + n] = value
            return carry

        lax.fori_loop(0, short_steps, step, tuple(old))


def medium_part(groups, ps, fb, qs, gs, ls, yb):
    for g in range(groups):
        for n in range(parts_of):
            begin = -1 if n in early else 0
            totals = {}
            for j in range(short_taps):
                tap = fb[g, n, j]
                for i in range(begin, short_steps):
                    term = tap * ps[g, n, short_taps + i - j]
                    totals[i] = term if j == 0 else totals[i] + term
            for i in range(begin, short_steps):
                yb[n, i + 1] = totals[i]

        def half(which, i):
            even, odd, both = halves[which]
            n = i // 2
            if i % 2 == 0:
                return yb[even, n + 1] + yb[odd, n]
            return yb[both, n + 1] - yb[even, n + 1] - yb[odd, n + 1]

        before = half(1, -1)
        for m in range(steps // 2):
            evens, odds, both = half(0, m), half(1, m), half(2, m)
            for r, medium in ((2 * m, evens + before), (2 * m + 1, both - evens - odds)):
                mixed = (qs[g, r] * medium).astype(jnp.bfloat16).astype(jnp.float32)
                gate = gate_at(gs, groups, g, 1, r)
                ls[g, r] = (gate * mixed).astype(jnp.bfloat16).astype(jnp.float32)
            before = odds


def long_part(groups, modes, k, ls, lam, skb, pw, carry_ref, ys, inits):
    sub = sublane()
    for g in range(groups):

        def step(r, states):
            value = ls[g, r]
            total = skb[g] * value
            after = []
            for m in range(modes):
                state = lam[0, g, m] * states[m] + value
                total = total + lam[1, g, m] * state
                after.append(state)
            ys[k, g, r] = total
            return tuple(after)

        zero = jnp.zeros((segs, lanes), jnp.float32)
        ends = lax.fori_loop(0, steps, step, (zero,) * modes, unroll=2)
        for m in range(modes):
            scan = ends[m]
            for n in range(3):
                scan = scan + jnp.where(
                    sub >= 1 << n, pw[n, g, m] * pltpu.roll(scan, 1 << n, 0), 0.0
                )
            carry = carry_ref[g, m]
            inits[k, g, m] = (
                jnp.where(sub == 0, 0.0, pltpu.roll(scan, 1, 0)) + pw[4, g, m] * carry
            )
            carry_ref[g, m] = fill(scan[segs - 1 : segs]) + pw[3, g, m] * carry


def finish_part(groups, modes, k, incoming, lam, pw, ys, inits, gs, outs):
    for g in range(groups):
        starts = []
        for m in range(modes):
            start = incoming[g, m]
            starts.append(lam[1, g, m] * (inits[k, g, m] + pw[4, g, m] * start))
            incoming[g, m] = pw[3, g, m] * start

        def step(r, states):
            total = ys[k, g, r]
            after = []
            for m in range(modes):
                state = lam[0, g, m] * states[m]
                total = total + state
                after.append(state)
            outs[g, pl.ds(pl.multiple_of(r * segs, segs), segs), :] = gate_at(gs, groups, g, 0, r) * total
            return tuple(after)

        lax.fori_loop(0, steps, step, tuple(starts), unroll=2)


def load_gates(k, gates, gs):
    rows = chunk * 4
    gs[...] = gates[pl.ds(pl.multiple_of(k * rows, rows), rows), :].astype(jnp.float32)


def gate_at(gs, groups, g, which, r):
    return gs[pl.ds((r * groups + g) * 2 + which, segs, stride=steps * groups * 2), :]


MESH = pl.DeviceIdType.MESH
kinds = 10
waits = 8
unit = 128
part_rows = 24


def place_of(owner):
    return lax.rem(owner, 2) * 8 + lax.rem(owner // 2, 2) * 4 + owner // 4


class Mover:
    def __init__(self, units, resid_ref, own_rows, rows_ref, send_sem, recv_sem, own_sem):
        self.units = units
        self.resid, self.own_rows, self.rows = resid_ref, own_rows, rows_ref
        self.send_sem, self.recv_sem, self.own_sem = send_sem, recv_sem, own_sem
        me = lax.axis_index("chan")
        core, pair, x = lax.rem(me, 2), lax.rem(me // 2, 2), me // 4
        right, left, far = lax.rem(x + 1, 4), lax.rem(x + 3, 4), lax.rem(x + 2, 4)
        other = 1 - pair

        def block(x, y):
            return core * 8 + y * 4 + x

        def device(x, y):
            return x * 4 + y * 2 + core

        self.here = block(x, pair)
        whole, first, second = (0, unit), (0, unit // 2), (unit // 2, unit // 2)
        east, west, across = device(right, pair), device(left, pair), device(x, other)
        twin = me + 1 - 2 * core
        self.table = (
            (east, block(x, pair), whole, 1, 0),
            (west, block(x, pair), whole, 1, 1),
            (across, block(x, pair), whole, 1, 2),
            (east, block(left, pair), first, 1, 3),
            (west, block(right, pair), second, 1, 3),
            (east, block(x, other), whole, 1, 4),
            (west, block(x, other), whole, 1, 5),
            (across, block(far, pair), whole, 1, 6),
            (twin, block(0, pair), whole, 4, 7),
            (twin, block(0, other), whole, 4, 7),
        )
        self.landing = (
            (block(left, pair), 1),
            (block(right, pair), 1),
            (block(x, other), 1),
            (block(far, pair), 1),
            (block(left, other), 1),
            (block(right, other), 1),
            (block(far, other), 1),
            ((1 - core) * 8, 8),
        )
        self.twin = twin

    def token_rows(self, q):
        first = lax.rem(q + self.units - chunk // unit, self.units)
        return pl.ds(pl.multiple_of(first * unit, unit), unit)

    def place(self, q, begin, count, owner, blocks):
        rows = pl.ds(pl.multiple_of(lax.rem(q, chunk // unit) * unit + begin, count), count)
        cols = pl.ds(pl.multiple_of(owner * 256, 256), blocks * 256)
        return self.rows.at[q // (chunk // unit), rows, cols]

    def remote(self, source, target_ref, kind, q, wait, target):
        return pltpu.make_async_remote_copy(
            src_ref=source,
            dst_ref=target_ref,
            send_sem=self.send_sem.at[kind],
            recv_sem=self.recv_sem.at[q, wait],
            device_id={"chan": target},
            device_id_type=MESH,
        )

    def start(self, q, *which):
        for kind in which:
            target, sent, (begin, count), blocks, wait = self.table[kind]
            place = self.place(q, begin, count, sent, blocks)
            source = self.resid.at[self.token_rows(q), :] if kind < 3 else place
            self.remote(source, place, kind, q, wait, target).start()

    def sent(self):
        for kind in range(kinds):
            _, _, (_, count), blocks, _ = self.table[kind]
            if blocks == 1:
                whole = self.own_rows.at[pl.ds(0, self.units * count), :]
            else:
                whole = self.rows.at[:, :, pl.ds(0, blocks * 256)]
            self.remote(whole, whole, kind, 0, 0, self.twin).wait_send()

    def arrived(self, q, *which):
        for wait in which:
            owner, blocks = self.landing[wait]
            place = self.place(q, 0, unit, owner, blocks)
            self.remote(place, place, 0, q, wait, self.twin).wait_recv()

    def own(self, q):
        return pltpu.make_async_copy(
            self.resid.at[self.token_rows(q), :],
            self.place(q, 0, unit, self.here, 1),
            self.own_sem.at[q],
        )

    def stage_1(self, q):
        self.start(q, 0, 1, 2)
        self.own(q).start()

    def stage_2(self, q):
        self.arrived(q, 0)
        self.start(q, 3)
        self.arrived(q, 1)
        self.start(q, 4)
        self.arrived(q, 2)
        self.start(q, 5, 6)

    def stage_3(self, q):
        self.own(q).wait()
        self.arrived(q, 3)
        self.start(q, 7, 8)

    def stage_4(self, q):
        self.arrived(q, 4, 5, 6)
        self.start(q, 9)

    def stage_5(self, q):
        self.arrived(q, 7)

    def tick(self, t):
        stages = ((5, self.stage_3), (8, self.stage_2), (11, self.stage_1), (3, self.stage_4))
        for lead, stage in stages:
            if isinstance(t, int):
                if 0 <= t + lead < self.units:
                    stage(t + lead)
            else:
                pl.when(t + lead < self.units)(functools.partial(stage, t + lead))


def scale_weights(groups, begin, end, parts, wts):
    def body(j, c):
        for h in range(2):
            row = parts[j, 16 + h : 17 + h, :]
            column = jnp.transpose(jnp.broadcast_to(row, (lanes, lanes)))
            rows = pl.ds(pl.multiple_of(j * 256 + h * lanes, lanes), lanes)
            for s in range(3):
                for g in range(groups):
                    value = wts[s, rows, lane_tile(g)].astype(jnp.float32)
                    wts[s, rows, lane_tile(g)] = (value * column).astype(jnp.bfloat16)
        return c

    lax.fori_loop(begin, end, body, 0)


def square_rows(tokens, own_rows, parts, me):
    def body(i, c):
        value = own_rows[pl.ds(pl.multiple_of(i * lanes, lanes), lanes), :].astype(jnp.float32)
        total = jnp.zeros((lanes, lanes), jnp.float32)
        for g in range(value.shape[1] // lanes):
            total = total + value[:, lane_tile(g)] * value[:, lane_tile(g)]
        parts[me, pl.ds(i, 1), :] = jnp.sum(jnp.transpose(total), axis=0, keepdims=True)
        return c

    lax.fori_loop(0, tokens // lanes, body, 0)


def project(groups, q, first, rows_ref, wts, scales, pj):
    columns_of = [
        jnp.transpose(jnp.broadcast_to(scales[pl.ds(first + h, 1), :], (lanes, lanes)))
        for h in range(chunk // lanes)
    ]
    for s in range(3):
        value = jnp.dot(rows_ref[q], wts[s], preferred_element_type=jnp.float32)
        for g in range(groups):
            for h, scale in enumerate(columns_of):
                piece = value[lane_tile(h), lane_tile(g)] * scale
                pj[s * groups + g, lane_tile(h), :] = piece.astype(jnp.bfloat16).astype(jnp.float32)


def fused_kernel(
    groups, modes, chunks, sides, peers,
    resid_ref, weight_hbm, gates_hbm, gain_ref, sf_ref, mr_ref, decay_ref, residue_ref, skip_ref,
    out_ref,
    rows_ref, wts, gates, own_rows, parts, scales, pj, pj_last, halo_in, tail_in, states, outs,
    tail, sfb, qs, ps, yb, fb, gs, ls, lam, skb, pw, carry_ref, incoming, ys, inits,
    send_sem, recv_sem, own_sem, gain_send, gain_recv, state_send, state_recv, halo_sem, weight_sem, own_load_sem, gates_sem,
):
    me, part = lax.axis_index("chan"), lax.axis_index("seq")
    own_load = pltpu.make_async_copy(resid_ref, own_rows, own_load_sem)
    own_load.start()
    load = pltpu.make_async_copy(weight_hbm, wts, weight_sem)
    for p in range(sides):
        owner = (p % 4) * 4 + (p % 8 // 4) * 2 + p // 8
        pltpu.make_async_copy(
            weight_hbm.at[:, owner * 256 : (owner + 1) * 256, :],
            wts.at[:, p * 256 : (p + 1) * 256, :],
            weight_sem,
        ).start()
    gates_load = pltpu.make_async_copy(gates_hbm, gates, gates_sem)
    gates_load.start()

    barrier = pltpu.get_barrier_semaphore()
    for o in range(1, sides):
        pl.semaphore_signal(barrier, inc=1, device_id={"chan": lax.rem(me + o, sides)}, device_id_type=MESH)
    for o in range(1, peers):
        pl.semaphore_signal(barrier, inc=1, device_id={"seq": lax.rem(part + o, peers)}, device_id_type=MESH)
    units = chunks * chunk // unit
    mover = Mover(units, resid_ref, own_rows, rows_ref, send_sem, recv_sem, own_sem)
    pl.semaphore_wait(barrier, sides + peers - 2)
    mover.tick(-11)
    mover.tick(-10)
    mover.tick(-9)

    gain = gain_ref[...].reshape(1, 256).astype(jnp.float32)
    parts[mover.here, 16:17, :] = gain[:, lane_tile(0)]
    parts[mover.here, 17:18, :] = gain[:, lane_tile(1)]
    own_load.wait()
    square_rows(chunks * chunk, own_rows, parts, mover.here)
    mover.tick(-8)

    def part_copy(o):
        return pltpu.make_async_remote_copy(
            src_ref=parts.at[mover.here], dst_ref=parts.at[mover.here],
            send_sem=gain_send.at[o], recv_sem=gain_recv.at[o],
            device_id={"chan": lax.rem(me + o, sides)}, device_id_type=MESH,
        )

    for o in range(1, sides):
        part_copy(o).start()
    mover.tick(-7)
    skip = skip_ref[...].reshape(1, 256)
    set_constants(groups, modes, sf_ref, mr_ref, decay_ref, residue_ref, skip, sfb, fb, lam, skb, pw)
    mover.tick(-6)
    carry_ref[...] = jnp.zeros_like(carry_ref)
    tail[...] = jnp.zeros_like(tail)
    ps[...] = jnp.zeros_like(ps)
    load.wait()
    gates_load.wait()
    mover.tick(-5)
    for o in range(1, sides):
        source = lax.rem(me + sides - o, sides)
        pltpu.make_async_remote_copy(
            src_ref=parts.at[place_of(source)], dst_ref=parts.at[place_of(source)],
            send_sem=gain_send.at[o], recv_sem=gain_recv.at[o],
            device_id={"chan": source}, device_id_type=MESH,
        ).wait_recv()
    squares = parts[0, 0:16, :]
    for p in range(1, sides):
        squares = squares + parts[p, 0:16, :]
    scales[...] = lax.rsqrt(squares / (sides * 256) + norm_epsilon)
    mover.tick(-4)
    scale_weights(groups, 0, sides, parts, wts)
    mover.tick(-3)
    mover.tick(-2)

    def halo_copies():
        sent = (
            (ps.at[:, pl.ds(0, phases), pl.ds(short_taps, short_steps), pl.ds(segs - back, back), :], halo_in),
            (tail.at[:, :, pl.ds(0, 1), :], tail_in),
        )
        return [
            pltpu.make_async_remote_copy(
                src_ref=source, dst_ref=target,
                send_sem=halo_sem.at[2 * n], recv_sem=halo_sem.at[2 * n + 1],
                device_id={"seq": lax.rem(part + 1, peers)}, device_id_type=MESH,
            )
            for n, (source, target) in enumerate(sent)
        ]

    def body(q, c):
        @pl.when(q < chunks)
        def _():
            for h in range(chunk // unit):
                mover.stage_5(q * (chunk // unit) + h)

        mover.tick(2 * q - 1)

        @pl.when(q < chunks)
        def _():
            first = lax.rem(q + chunks - 1, chunks) * (chunk // lanes)
            project(groups, q, first, rows_ref, wts, scales, pj)

        @pl.when(q == 0)
        def _():
            pj_last[...] = pj[...]
            short_part(groups, pj, tail, sfb, qs, ps)
            for copy in halo_copies():
                copy.start()

        @pl.when(q == 1)
        def _():
            for copy in halo_copies():
                copy.wait()
            seen = jnp.where(part > 0, 1.0, 0.0)
            for g in range(groups):
                for i in range(phases):
                    for n in range(short_steps):
                        ps[g, i, short_taps + n, segs - back :, :] = halo_in[g, i, n] * seen
            for n in range(3 * groups):
                for i in range(2):
                    tail[n, i, 0:1, :] = tail_in[n, i] * seen

        @pl.when(q == chunks)
        def _():
            pj[...] = pj_last[...]

        @pl.when(q > 0)
        def _():
            short_part(groups, pj, tail, sfb, qs, ps)

        mover.tick(2 * q)

        @pl.when(q > 0)
        def _():
            k = q - 1
            load_gates(k, gates, gs)
            medium_part(groups, ps, fb, qs, gs, ls, yb)
            long_part(groups, modes, k, ls, lam, skb, pw, carry_ref, ys, inits)

        return c

    lax.fori_loop(0, chunks + 1, body, 0)

    for g in range(groups):
        for m in range(modes):
            states[0, g, m : m + 1, :] = carry_ref[g, m, 0:1, :]

    def state_copy(o):
        return pltpu.make_async_remote_copy(
            src_ref=states.at[0], dst_ref=states.at[o],
            send_sem=state_send.at[o], recv_sem=state_recv.at[o],
            device_id={"seq": lax.rem(part + o, peers)}, device_id_type=MESH,
        )

    for o in range(1, peers):
        state_copy(o).start()

    mover.sent()
    for o in range(1, sides):
        part_copy(o).wait_send()
    for o in range(1, peers):
        state_copy(o).wait()
    for g in range(groups):
        total = jnp.zeros((modes, lanes), jnp.float32)
        d = decay_ref[:, lane_tile(g)]
        for o in range(1, peers):
            weight = jnp.exp(d * (-1.0 * chunk * chunks * (o - 1)))
            total = total + jnp.where(part >= o, weight, 0.0) * states[o, g]
        for m in range(modes):
            incoming[g, m] = fill(total[m : m + 1])

    def finish(k, c):
        load_gates(k, gates, gs)
        finish_part(groups, modes, k, incoming, lam, pw, ys, inits, gs, outs)
        for g in range(groups):
            for seg in range(segs):
                for r in range(0, steps, 16):
                    pieces = [
                        outs[g, pl.ds((r + half) * segs + seg, 8, stride=segs), :] for half in (0, 8)
                    ]
                    rows = pl.ds(pl.multiple_of(k * chunk + seg * steps + r, 16), 16)
                    out_ref[rows, lane_tile(g)] = jnp.concatenate(pieces, axis=0).astype(jnp.bfloat16)
        return c

    lax.fori_loop(0, chunks, finish, 0)


def in_vmem(n):
    return [pl.BlockSpec(memory_space=pltpu.VMEM)] * n


def vregs(*lead):
    return pltpu.VMEM(lead + (segs, lanes), jnp.float32)


def fused_call(resid, weight, gates, gain, short_filter, mr_filter, decays, residue, skip):
    length, width = resid.shape
    modes = decays.shape[0]
    groups, chunks = width // lanes, length // chunk
    sides, peers = lax.axis_size("chan"), lax.axis_size("seq")
    units = length // unit
    f32, bf16 = jnp.float32, jnp.bfloat16
    dma = pltpu.SemaphoreType.DMA
    anywhere = pl.BlockSpec(memory_space=pl.ANY)
    vmem = pl.BlockSpec(memory_space=pltpu.VMEM)
    return pl.pallas_call(
        functools.partial(fused_kernel, groups, modes, chunks, sides, peers),
        out_shape=jax.ShapeDtypeStruct((length, width), bf16),
        in_specs=[anywhere] * 3 + [vmem] * 6,
        out_specs=vmem,
        scratch_shapes=[
            pltpu.VMEM((chunks, chunk, sides * width), bf16),
            pltpu.VMEM((3, sides * width, width), bf16),
            pltpu.VMEM(gates.shape, bf16),
            pltpu.VMEM((length, width), bf16),
            pltpu.VMEM((sides, part_rows, lanes), f32),
            pltpu.VMEM((length // lanes, lanes), f32),
            pltpu.VMEM((3 * groups, chunk, lanes), f32),
            pltpu.VMEM((3 * groups, chunk, lanes), f32),
            pltpu.VMEM((groups, phases, short_steps, back, lanes), f32),
            pltpu.VMEM((3 * groups, 2, 1, lanes), f32),
            pltpu.VMEM((peers, groups, modes, lanes), f32),
            pltpu.VMEM((groups, chunk, lanes), f32),
            vregs(3 * groups, 2),
            vregs(9 * groups),
            vregs(groups, steps),
            vregs(groups, parts_of, short_taps + short_steps),
            vregs(parts_of, short_steps + 1),
            vregs(groups, parts_of, short_taps),
            pltpu.VMEM((chunk * 2 * groups, lanes), f32),
            vregs(groups, steps),
            vregs(2, groups, modes),
            vregs(groups),
            vregs(5, groups, modes),
            vregs(groups, modes),
            vregs(groups, modes),
            vregs(chunks, groups, steps),
            vregs(chunks, groups, modes),
            dma((kinds,)),
            dma((units, waits)),
            dma((units,)),
            dma((sides,)),
            dma((sides,)),
            dma((peers,)),
            dma((peers,)),
            dma((4,)),
            dma,
            dma,
            dma,
        ],
        compiler_params=pltpu.CompilerParams(
            vmem_limit_bytes=60 << 20, collective_id=0, has_side_effects=True
        ),
    )(resid, weight, gates, gain, short_filter, mr_filter, decays, residue, skip)


def on_device(
    resid, norm_gain, feat_weight, short_filter, mr_filter, gates_lr, decay_rate, residue, skip_gain
):
    tokens, two, width = gates_lr.shape
    gates = gates_lr.reshape(tokens, two, width // lanes, lanes).transpose(0, 2, 1, 3)
    return fused_call(
        resid,
        jnp.transpose(feat_weight, (1, 0, 2)),
        gates.reshape(tokens * two * (width // lanes), lanes),
        norm_gain,
        short_filter,
        mr_filter,
        decay_rate,
        residue,
        skip_gain,
    )


def solution(mesh):
    in_specs = (
        P("seq", "chan"),
        P("chan"),
        P(None, None, "chan"),
        P(None, None, "chan"),
        P(None, "chan"),
        P("seq", None, "chan"),
        P(None, "chan"),
        P(None, "chan"),
        P("chan"),
    )
    return jax.shard_map(
        on_device, mesh=mesh, in_specs=in_specs, out_specs=P("seq", "chan"), check_vma=False
    )
```

```python
import functools

import jax
import jax.numpy as jnp
from jax import lax
from jax.experimental import pallas as pl
from jax.experimental.pallas import tpu as pltpu
from jax.sharding import PartitionSpec as P

norm_epsilon = 1e-05
lanes = 128
segs = 8
steps = 32
chunk = segs * steps
taps = 128
back = taps // steps
phases = 4
short_steps = steps // phases
short_taps = taps // phases
sums = ((0, 2), (1, 3), (0, 1), (2, 3), (4, 5))
parts_of = phases + len(sums)
halves = ((0, 2, 4), (1, 3, 5), (6, 7, 8))
early = (1, 2, 3, 5, 7)


def sublane():
    return lax.broadcasted_iota(jnp.int32, (segs, lanes), 0)


def fill(row):
    return jnp.broadcast_to(row, (segs, lanes))


def lane_tile(i):
    return slice(i * lanes, (i + 1) * lanes)


def modal_weights(decay, residue):
    x = decay * 2.0
    small = x * (1.0 - x / 2.0 * (1.0 - x / 3.0 * (1.0 - x / 4.0 * (1.0 - x / 5.0 * (1.0 - x / 6.0)))))
    return residue * jnp.sqrt(jnp.where(x < 0.125, small, 1.0 - jnp.exp(-x)))


def set_constants(groups, modes, sf_ref, mr_ref, decay_ref, residue_ref, skip, sfb, fb, lam, skb, pw):
    for g in range(groups):
        cols = lane_tile(g)
        for s in range(3):
            for j in range(3):
                sfb[(s * groups + g) * 3 + j] = fill(sf_ref[j, s : s + 1, cols])
        skb[g] = fill(skip[:, cols])

        def taps_at(t, carry):
            rows = mr_ref[pl.ds(pl.multiple_of(t * 16, 16), 16), cols].astype(jnp.float32)
            for j in range(16 // phases):
                values = [fill(rows[phases * j + i : phases * j + i + 1]) for i in range(phases)]
                for a, b in sums:
                    values.append(values[a] + values[b])
                for n, value in enumerate(values):
                    fb[g, n, t * (16 // phases) + j] = value
            return carry

        lax.fori_loop(0, taps // 16, taps_at, 0)
        at = sublane().astype(jnp.float32) * float(steps)
        modal = modal_weights(decay_ref[:, cols], residue_ref[:, cols])
        for m in range(modes):
            d = fill(decay_ref[m : m + 1, cols])
            lam[0, g, m] = jnp.exp(-d)
            lam[1, g, m] = fill(modal[m : m + 1])
            pw[0, g, m] = jnp.exp(d * (-1.0 * steps))
            pw[1, g, m] = jnp.exp(d * (-2.0 * steps))
            pw[2, g, m] = jnp.exp(d * (-4.0 * steps))
            pw[3, g, m] = jnp.exp(d * (-8.0 * steps))
            pw[4, g, m] = jnp.exp(-d * at)


def strided(ref, lead, r):
    return ref[lead, pl.ds(r, segs, stride=steps), :]


def short_part(groups, pj, tail, sfb, qs, ps):
    sub = sublane()
    for g in range(groups):
        names = [s * groups + g for s in range(3)]
        old = []
        for n in names:
            last = strided(pj, n, steps - 1)
            before = strided(pj, n, steps - 2)
            turned = (pltpu.roll(last, 1, 0), pltpu.roll(before, 1, 0))
            old.append(
                (
                    jnp.where(sub == 0, tail[n, 0], turned[0]),
                    jnp.where(sub == 0, tail[n, 1], turned[1]),
                )
            )
            tail[n, 0] = turned[0]
            tail[n, 1] = turned[1]

        def step(n, carry):
            products = []
            for i in range(phases):
                r = n * phases + i
                after, featured = [], []
                for name, (one, two) in zip(names, carry):
                    now = strided(pj, name, r)
                    featured.append(
                        sfb[name * 3] * now + sfb[name * 3 + 1] * one + sfb[name * 3 + 2] * two
                    )
                    after.append((now, one))
                carry = tuple(after)
                products.append((featured[1] * featured[2]).astype(jnp.bfloat16).astype(jnp.float32))
                qs[g, r] = featured[0]
            past = [ps[g, i, short_taps + n] for i in range(phases)]
            for shift in range(back + 1):
                values = products
                if shift > 0:
                    values = [
                        pltpu.roll(jnp.where(sub >= segs - shift, old, new), shift, 0)
                        for old, new in zip(past, products)
                    ]
                values = list(values)
                for x, y in sums:
                    values.append(values[x] + values[y])
                for i, value in enumerate(values):
                    ps[g, i, short_taps - shift * short_steps + n] = value
            return carry

        lax.fori_loop(0, short_steps, step, tuple(old))


def medium_part(groups, ps, fb, qs, gs, ls, yb):
    for g in range(groups):
        for n in range(parts_of):
            begin = -1 if n in early else 0
            totals = {}
            for j in range(short_taps):
                tap = fb[g, n, j]
                for i in range(begin, short_steps):
                    term = tap * ps[g, n, short_taps + i - j]
                    totals[i] = term if j == 0 else totals[i] + term
            for i in range(begin, short_steps):
                yb[n, i + 1] = totals[i]

        def half(which, i):
            even, odd, both = halves[which]
            n = i // 2
            if i % 2 == 0:
                return yb[even, n + 1] + yb[odd, n]
            return yb[both, n + 1] - yb[even, n + 1] - yb[odd, n + 1]

        before = half(1, -1)
        for m in range(steps // 2):
            evens, odds, both = half(0, m), half(1, m), half(2, m)
            for r, medium in ((2 * m, evens + before), (2 * m + 1, both - evens - odds)):
                mixed = (qs[g, r] * medium).astype(jnp.bfloat16).astype(jnp.float32)
                gate = gate_at(gs, groups, g, 1, r)
                ls[g, r] = (gate * mixed).astype(jnp.bfloat16).astype(jnp.float32)
            before = odds


def long_part(groups, modes, k, ls, lam, skb, pw, carry_ref, ys, inits):
    sub = sublane()
    for g in range(groups):

        def step(r, states):
            value = ls[g, r]
            total = skb[g] * value
            after = []
            for m in range(modes):
                state = lam[0, g, m] * states[m] + value
                total = total + lam[1, g, m] * state
                after.append(state)
            ys[k, g, r] = total
            return tuple(after)

        zero = jnp.zeros((segs, lanes), jnp.float32)
        ends = lax.fori_loop(0, steps, step, (zero,) * modes, unroll=4)
        for m in range(modes):
            scan = ends[m]
            for n in range(3):
                scan = scan + jnp.where(
                    sub >= 1 << n, pw[n, g, m] * pltpu.roll(scan, 1 << n, 0), 0.0
                )
            carry = carry_ref[g, m]
            inits[k, g, m] = (
                jnp.where(sub == 0, 0.0, pltpu.roll(scan, 1, 0)) + pw[4, g, m] * carry
            )
            carry_ref[g, m] = fill(scan[segs - 1 : segs]) + pw[3, g, m] * carry


def finish_part(groups, modes, k, incoming, lam, pw, ys, inits, gs, outs):
    for g in range(groups):
        starts = []
        for m in range(modes):
            start = incoming[g, m]
            starts.append(lam[1, g, m] * (inits[k, g, m] + pw[4, g, m] * start))
            incoming[g, m] = pw[3, g, m] * start

        def step(r, states):
            total = ys[k, g, r]
            after = []
            for m in range(modes):
                state = lam[0, g, m] * states[m]
                total = total + state
                after.append(state)
            outs[g, pl.ds(pl.multiple_of(r * segs, segs), segs), :] = gate_at(gs, groups, g, 0, r) * total
            return tuple(after)

        lax.fori_loop(0, steps, step, tuple(starts), unroll=4)


def load_gates(k, gates, gs):
    rows = chunk * 4
    gs[...] = gates[pl.ds(pl.multiple_of(k * rows, rows), rows), :].astype(jnp.float32)


def gate_at(gs, groups, g, which, r):
    return gs[pl.ds((r * groups + g) * 2 + which, segs, stride=steps * groups * 2), :]


MESH = pl.DeviceIdType.MESH
kinds = 10
waits = 8
unit = 128
part_rows = 24


def place_of(owner):
    return lax.rem(owner, 2) * 8 + lax.rem(owner // 2, 2) * 4 + owner // 4


class Mover:
    def __init__(self, units, resid_ref, own_rows, rows_ref, send_sem, recv_sem, own_sem):
        self.units = units
        self.resid, self.own_rows, self.rows = resid_ref, own_rows, rows_ref
        self.send_sem, self.recv_sem, self.own_sem = send_sem, recv_sem, own_sem
        me = lax.axis_index("chan")
        core, pair, x = lax.rem(me, 2), lax.rem(me // 2, 2), me // 4
        right, left, far = lax.rem(x + 1, 4), lax.rem(x + 3, 4), lax.rem(x + 2, 4)
        other = 1 - pair

        def block(x, y):
            return core * 8 + y * 4 + x

        def device(x, y):
            return x * 4 + y * 2 + core

        self.here = block(x, pair)
        whole, first, second = (0, unit), (0, unit // 2), (unit // 2, unit // 2)
        east, west, across = device(right, pair), device(left, pair), device(x, other)
        twin = me + 1 - 2 * core
        self.table = (
            (east, block(x, pair), whole, 1, 0),
            (west, block(x, pair), whole, 1, 1),
            (across, block(x, pair), whole, 1, 2),
            (east, block(left, pair), first, 1, 3),
            (west, block(right, pair), second, 1, 3),
            (east, block(x, other), whole, 1, 4),
            (west, block(x, other), whole, 1, 5),
            (across, block(far, pair), whole, 1, 6),
            (twin, block(0, pair), whole, 4, 7),
            (twin, block(0, other), whole, 4, 7),
        )
        self.landing = (
            (block(left, pair), 1),
            (block(right, pair), 1),
            (block(x, other), 1),
            (block(far, pair), 1),
            (block(left, other), 1),
            (block(right, other), 1),
            (block(far, other), 1),
            ((1 - core) * 8, 8),
        )
        self.twin = twin

    def token_rows(self, q):
        first = lax.rem(q + self.units - chunk // unit, self.units)
        return pl.ds(pl.multiple_of(first * unit, unit), unit)

    def place(self, q, begin, count, owner, blocks):
        rows = pl.ds(pl.multiple_of(lax.rem(q, chunk // unit) * unit + begin, count), count)
        cols = pl.ds(pl.multiple_of(owner * 256, 256), blocks * 256)
        return self.rows.at[q // (chunk // unit), rows, cols]

    def remote(self, source, target_ref, kind, q, wait, target):
        return pltpu.make_async_remote_copy(
            src_ref=source,
            dst_ref=target_ref,
            send_sem=self.send_sem.at[kind],
            recv_sem=self.recv_sem.at[q, wait],
            device_id={"chan": target},
            device_id_type=MESH,
        )

    def start(self, q, *which):
        for kind in which:
            target, sent, (begin, count), blocks, wait = self.table[kind]
            place = self.place(q, begin, count, sent, blocks)
            source = self.resid.at[self.token_rows(q), :] if kind < 3 else place
            self.remote(source, place, kind, q, wait, target).start()

    def sent(self):
        for kind in range(kinds):
            _, _, (_, count), blocks, _ = self.table[kind]
            if blocks == 1:
                whole = self.own_rows.at[pl.ds(0, self.units * count), :]
            else:
                whole = self.rows.at[:, :, pl.ds(0, blocks * 256)]
            self.remote(whole, whole, kind, 0, 0, self.twin).wait_send()

    def arrived(self, q, *which):
        for wait in which:
            owner, blocks = self.landing[wait]
            place = self.place(q, 0, unit, owner, blocks)
            self.remote(place, place, 0, q, wait, self.twin).wait_recv()

    def own(self, q):
        return pltpu.make_async_copy(
            self.resid.at[self.token_rows(q), :],
            self.place(q, 0, unit, self.here, 1),
            self.own_sem.at[q],
        )

    def stage_1(self, q):
        self.start(q, 0, 1, 2)
        self.own(q).start()

    def stage_2(self, q):
        self.arrived(q, 0)
        self.start(q, 3)
        self.arrived(q, 1)
        self.start(q, 4)
        self.arrived(q, 2)
        self.start(q, 5, 6)

    def stage_3(self, q):
        self.own(q).wait()
        self.arrived(q, 3)
        self.start(q, 7, 8)

    def stage_4(self, q):
        self.arrived(q, 4, 5, 6)
        self.start(q, 9)

    def stage_5(self, q):
        self.arrived(q, 7)

    def tick(self, t):
        stages = ((5, self.stage_3), (8, self.stage_2), (11, self.stage_1), (3, self.stage_4))
        for lead, stage in stages:
            if isinstance(t, int):
                if 0 <= t + lead < self.units:
                    stage(t + lead)
            else:
                pl.when(t + lead < self.units)(functools.partial(stage, t + lead))


def scale_weights(groups, begin, end, parts, wts):
    def body(j, c):
        for h in range(2):
            row = parts[j, 16 + h : 17 + h, :]
            column = jnp.transpose(jnp.broadcast_to(row, (lanes, lanes)))
            rows = pl.ds(pl.multiple_of(j * 256 + h * lanes, lanes), lanes)
            for s in range(3):
                for g in range(groups):
                    value = wts[s, rows, lane_tile(g)].astype(jnp.float32)
                    wts[s, rows, lane_tile(g)] = (value * column).astype(jnp.bfloat16)
        return c

    lax.fori_loop(begin, end, body, 0)


def square_rows(tokens, own_rows, parts, me):
    def body(i, c):
        value = own_rows[pl.ds(pl.multiple_of(i * lanes, lanes), lanes), :].astype(jnp.float32)
        total = jnp.zeros((lanes, lanes), jnp.float32)
        for g in range(value.shape[1] // lanes):
            total = total + value[:, lane_tile(g)] * value[:, lane_tile(g)]
        parts[me, pl.ds(i, 1), :] = jnp.sum(jnp.transpose(total), axis=0, keepdims=True)
        return c

    lax.fori_loop(0, tokens // lanes, body, 0)


def project(groups, q, first, rows_ref, wts, scales, pj):
    columns_of = [
        jnp.transpose(jnp.broadcast_to(scales[pl.ds(first + h, 1), :], (lanes, lanes)))
        for h in range(chunk // lanes)
    ]
    for s in range(3):
        value = jnp.dot(rows_ref[q], wts[s], preferred_element_type=jnp.float32)
        for g in range(groups):
            for h, scale in enumerate(columns_of):
                piece = value[lane_tile(h), lane_tile(g)] * scale
                pj[s * groups + g, lane_tile(h), :] = piece.astype(jnp.bfloat16).astype(jnp.float32)


def fused_kernel(
    groups, modes, chunks, sides, peers,
    resid_ref, weight_hbm, gates_hbm, gain_ref, sf_ref, mr_ref, decay_ref, residue_ref, skip_ref,
    out_ref,
    rows_ref, wts, gates, own_rows, parts, scales, pj, pj_last, halo_in, tail_in, states, outs,
    tail, sfb, qs, ps, yb, fb, gs, ls, lam, skb, pw, carry_ref, incoming, ys, inits,
    send_sem, recv_sem, own_sem, gain_send, gain_recv, state_send, state_recv, halo_sem, weight_sem, own_load_sem, gates_sem,
):
    me, part = lax.axis_index("chan"), lax.axis_index("seq")
    own_load = pltpu.make_async_copy(resid_ref, own_rows, own_load_sem)
    own_load.start()
    load = pltpu.make_async_copy(weight_hbm, wts, weight_sem)
    for p in range(sides):
        owner = (p % 4) * 4 + (p % 8 // 4) * 2 + p // 8
        pltpu.make_async_copy(
            weight_hbm.at[:, owner * 256 : (owner + 1) * 256, :],
            wts.at[:, p * 256 : (p + 1) * 256, :],
            weight_sem,
        ).start()
    gates_load = pltpu.make_async_copy(gates_hbm, gates, gates_sem)
    gates_load.start()

    barrier = pltpu.get_barrier_semaphore()
    for o in range(1, sides):
        pl.semaphore_signal(barrier, inc=1, device_id={"chan": lax.rem(me + o, sides)}, device_id_type=MESH)
    for o in range(1, peers):
        pl.semaphore_signal(barrier, inc=1, device_id={"seq": lax.rem(part + o, peers)}, device_id_type=MESH)
    units = chunks * chunk // unit
    mover = Mover(units, resid_ref, own_rows, rows_ref, send_sem, recv_sem, own_sem)
    pl.semaphore_wait(barrier, sides + peers - 2)
    mover.tick(-11)
    mover.tick(-10)
    mover.tick(-9)

    gain = gain_ref[...].reshape(1, 256).astype(jnp.float32)
    parts[mover.here, 16:17, :] = gain[:, lane_tile(0)]
    parts[mover.here, 17:18, :] = gain[:, lane_tile(1)]
    own_load.wait()
    square_rows(chunks * chunk, own_rows, parts, mover.here)
    mover.tick(-8)

    def part_copy(o):
        return pltpu.make_async_remote_copy(
            src_ref=parts.at[mover.here], dst_ref=parts.at[mover.here],
            send_sem=gain_send.at[o], recv_sem=gain_recv.at[o],
            device_id={"chan": lax.rem(me + o, sides)}, device_id_type=MESH,
        )

    for o in range(1, sides):
        part_copy(o).start()
    mover.tick(-7)
    skip = skip_ref[...].reshape(1, 256)
    set_constants(groups, modes, sf_ref, mr_ref, decay_ref, residue_ref, skip, sfb, fb, lam, skb, pw)
    mover.tick(-6)
    carry_ref[...] = jnp.zeros_like(carry_ref)
    tail[...] = jnp.zeros_like(tail)
    ps[...] = jnp.zeros_like(ps)
    load.wait()
    gates_load.wait()
    mover.tick(-5)
    for o in range(1, sides):
        source = lax.rem(me + sides - o, sides)
        pltpu.make_async_remote_copy(
            src_ref=parts.at[place_of(source)], dst_ref=parts.at[place_of(source)],
            send_sem=gain_send.at[o], recv_sem=gain_recv.at[o],
            device_id={"chan": source}, device_id_type=MESH,
        ).wait_recv()
    squares = parts[0, 0:16, :]
    for p in range(1, sides):
        squares = squares + parts[p, 0:16, :]
    scales[...] = lax.rsqrt(squares / (sides * 256) + norm_epsilon)
    mover.tick(-4)
    scale_weights(groups, 0, sides, parts, wts)
    mover.tick(-3)
    mover.tick(-2)

    def halo_copies():
        sent = (
            (ps.at[:, pl.ds(0, phases), pl.ds(short_taps, short_steps), pl.ds(segs - back, back), :], halo_in),
            (tail.at[:, :, pl.ds(0, 1), :], tail_in),
        )
        return [
            pltpu.make_async_remote_copy(
                src_ref=source, dst_ref=target,
                send_sem=halo_sem.at[2 * n], recv_sem=halo_sem.at[2 * n + 1],
                device_id={"seq": lax.rem(part + 1, peers)}, device_id_type=MESH,
            )
            for n, (source, target) in enumerate(sent)
        ]

    def body(q, c):
        @pl.when(q < chunks)
        def _():
            for h in range(chunk // unit):
                mover.stage_5(q * (chunk // unit) + h)

        mover.tick(2 * q - 1)

        @pl.when(q < chunks)
        def _():
            first = lax.rem(q + chunks - 1, chunks) * (chunk // lanes)
            project(groups, q, first, rows_ref, wts, scales, pj)

        @pl.when(q == 0)
        def _():
            pj_last[...] = pj[...]
            short_part(groups, pj, tail, sfb, qs, ps)
            for copy in halo_copies():
                copy.start()

        @pl.when(q == 1)
        def _():
            for copy in halo_copies():
                copy.wait()
            seen = jnp.where(part > 0, 1.0, 0.0)
            for g in range(groups):
                for i in range(phases):
                    for n in range(short_steps):
                        ps[g, i, short_taps + n, segs - back :, :] = halo_in[g, i, n] * seen
            for n in range(3 * groups):
                for i in range(2):
                    tail[n, i, 0:1, :] = tail_in[n, i] * seen

        @pl.when(q == chunks)
        def _():
            pj[...] = pj_last[...]

        @pl.when(q > 0)
        def _():
            short_part(groups, pj, tail, sfb, qs, ps)

        mover.tick(2 * q)

        @pl.when(q > 0)
        def _():
            k = q - 1
            load_gates(k, gates, gs)
            medium_part(groups, ps, fb, qs, gs, ls, yb)
            long_part(groups, modes, k, ls, lam, skb, pw, carry_ref, ys, inits)

        return c

    lax.fori_loop(0, chunks + 1, body, 0)

    for g in range(groups):
        for m in range(modes):
            states[0, g, m : m + 1, :] = carry_ref[g, m, 0:1, :]

    def state_copy(o):
        return pltpu.make_async_remote_copy(
            src_ref=states.at[0], dst_ref=states.at[o],
            send_sem=state_send.at[o], recv_sem=state_recv.at[o],
            device_id={"seq": lax.rem(part + o, peers)}, device_id_type=MESH,
        )

    for o in range(1, peers):
        state_copy(o).start()

    mover.sent()
    for o in range(1, sides):
        part_copy(o).wait_send()
    for o in range(1, peers):
        state_copy(o).wait()
    for g in range(groups):
        total = jnp.zeros((modes, lanes), jnp.float32)
        d = decay_ref[:, lane_tile(g)]
        for o in range(1, peers):
            weight = jnp.exp(d * (-1.0 * chunk * chunks * (o - 1)))
            total = total + jnp.where(part >= o, weight, 0.0) * states[o, g]
        for m in range(modes):
            incoming[g, m] = fill(total[m : m + 1])

    def finish(k, c):
        load_gates(k, gates, gs)
        finish_part(groups, modes, k, incoming, lam, pw, ys, inits, gs, outs)
        for g in range(groups):
            for seg in range(segs):
                for r in range(0, steps, 16):
                    pieces = [
                        outs[g, pl.ds((r + half) * segs + seg, 8, stride=segs), :] for half in (0, 8)
                    ]
                    rows = pl.ds(pl.multiple_of(k * chunk + seg * steps + r, 16), 16)
                    out_ref[rows, lane_tile(g)] = jnp.concatenate(pieces, axis=0).astype(jnp.bfloat16)
        return c

    lax.fori_loop(0, chunks, finish, 0)


def in_vmem(n):
    return [pl.BlockSpec(memory_space=pltpu.VMEM)] * n


def vregs(*lead):
    return pltpu.VMEM(lead + (segs, lanes), jnp.float32)


def fused_call(resid, weight, gates, gain, short_filter, mr_filter, decays, residue, skip):
    length, width = resid.shape
    modes = decays.shape[0]
    groups, chunks = width // lanes, length // chunk
    sides, peers = lax.axis_size("chan"), lax.axis_size("seq")
    units = length // unit
    f32, bf16 = jnp.float32, jnp.bfloat16
    dma = pltpu.SemaphoreType.DMA
    anywhere = pl.BlockSpec(memory_space=pl.ANY)
    vmem = pl.BlockSpec(memory_space=pltpu.VMEM)
    return pl.pallas_call(
        functools.partial(fused_kernel, groups, modes, chunks, sides, peers),
        out_shape=jax.ShapeDtypeStruct((length, width), bf16),
        in_specs=[anywhere] * 3 + [vmem] * 6,
        out_specs=vmem,
        scratch_shapes=[
            pltpu.VMEM((chunks, chunk, sides * width), bf16),
            pltpu.VMEM((3, sides * width, width), bf16),
            pltpu.VMEM(gates.shape, bf16),
            pltpu.VMEM((length, width), bf16),
            pltpu.VMEM((sides, part_rows, lanes), f32),
            pltpu.VMEM((length // lanes, lanes), f32),
            pltpu.VMEM((3 * groups, chunk, lanes), f32),
            pltpu.VMEM((3 * groups, chunk, lanes), f32),
            pltpu.VMEM((groups, phases, short_steps, back, lanes), f32),
            pltpu.VMEM((3 * groups, 2, 1, lanes), f32),
            pltpu.VMEM((peers, groups, modes, lanes), f32),
            pltpu.VMEM((groups, chunk, lanes), f32),
            vregs(3 * groups, 2),
            vregs(9 * groups),
            vregs(groups, steps),
            vregs(groups, parts_of, short_taps + short_steps),
            vregs(parts_of, short_steps + 1),
            vregs(groups, parts_of, short_taps),
            pltpu.VMEM((chunk * 2 * groups, lanes), f32),
            vregs(groups, steps),
            vregs(2, groups, modes),
            vregs(groups),
            vregs(5, groups, modes),
            vregs(groups, modes),
            vregs(groups, modes),
            vregs(chunks, groups, steps),
            vregs(chunks, groups, modes),
            dma((kinds,)),
            dma((units, waits)),
            dma((units,)),
            dma((sides,)),
            dma((sides,)),
            dma((peers,)),
            dma((peers,)),
            dma((4,)),
            dma,
            dma,
            dma,
        ],
        compiler_params=pltpu.CompilerParams(
            vmem_limit_bytes=60 << 20, collective_id=0, has_side_effects=True
        ),
    )(resid, weight, gates, gain, short_filter, mr_filter, decays, residue, skip)


def on_device(
    resid, norm_gain, feat_weight, short_filter, mr_filter, gates_lr, decay_rate, residue, skip_gain
):
    tokens, two, width = gates_lr.shape
    gates = gates_lr.reshape(tokens, two, width // lanes, lanes).transpose(0, 2, 1, 3)
    return fused_call(
        resid,
        jnp.transpose(feat_weight, (1, 0, 2)),
        gates.reshape(tokens * two * (width // lanes), lanes),
        norm_gain,
        short_filter,
        mr_filter,
        decay_rate,
        residue,
        skip_gain,
    )


def solution(mesh):
    in_specs = (
        P("seq", "chan"),
        P("chan"),
        P(None, None, "chan"),
        P(None, None, "chan"),
        P(None, "chan"),
        P("seq", None, "chan"),
        P(None, "chan"),
        P(None, "chan"),
        P("chan"),
    )
    return jax.shard_map(
        on_device, mesh=mesh, in_specs=in_specs, out_specs=P("seq", "chan"), check_vma=False
    )
```
